256 devices in a mesh: dp: 8 (over z), seq: 32 (over x, y, core).
Axes of the slice: x: 4, y: 4, z: 8, core: 2. Of those that a mesh axis runs over, the one named last changes fastest.
Arguments:
- tokens: bfloat16 [8, 4096, 1024], P('dp', 'seq'), may hold values from -6 to 6
- weights: bfloat16 [1024, 3072], replicated, may hold values from -0.1875 to 0.1875
- dout: bfloat16 [8, 4096, 1024], P('dp', 'seq'), may hold values from -6 to 6
Outputs:
- token_grad: bfloat16 [8, 4096, 1024], P('dp', 'seq')
- proj_grad: float32 [1024, 3072], P(('dp', 'seq'))
The draws below stay inside these ranges and needn't reach their ends.
All inputs are finite; a program needn't handle non-finite values.
Results may differ from the reference program's by a relative error of at most 0.007.
Values sent between devices are 32-bit elements; how exact they have to be, the bound alone decides.
A program may use at most 128 MiB of HBM per device.

```python
import math
import jax
import jax.numpy as jnp
from jax import lax

D = 1024
HEADS = 8
HD = 128
TOK_DEV = 128
E = 1024
SEQLEN = 4096
BATCH = 8


def spiked(result, stream_key, source, target, parts, factor):
    def block_of(dim):
        return (jnp.arange(result.shape[dim]) // (result.shape[dim] // parts)).reshape((-1,) + (1,) * (result.ndim - 1 - dim))

    near = jax.random.permutation(stream_key, parts)[block_of(target)]
    other_side = (block_of(target) + parts // 2) % parts
    return jnp.where((block_of(source) == near) | (block_of(source) == other_side), factor * result, result)


def levels(key, shape, split, least, high):
    def one(dim, parts):
        heights = jax.random.uniform(jax.random.fold_in(jax.random.fold_in(key, 6), dim), (parts,), jnp.float32, least / len(split), high / len(split))
        return jnp.repeat(jnp.exp(heights), shape[dim] // parts).reshape((-1,) + (1,) * (len(shape) - dim - 1))

    factor_of = one(*split[0])
    for cut in split[1:]:
        factor_of = factor_of * one(*cut)
    return factor_of


def normal_values(key, shape, spread, bound, cuts=(), held_as=jnp.bfloat16):
    result = spread * jax.random.normal(key, shape, jnp.float32)
    if cuts:
        result = result * levels(key, shape, cuts, -0.22, 0.18)
    return jnp.clip(result, -bound, bound).astype(held_as)


def gaussian_with(own_key, dims, scale, bound, cuts, heavy, kind=jnp.bfloat16):
    values = scale * jax.random.normal(own_key, dims, jnp.float32)
    if cuts:
        values = values * levels(own_key, dims, cuts, -0.22, 0.18)
    return jnp.clip(spiked(values, jax.random.fold_in(own_key, 3), *heavy), -bound, bound).astype(kind)


def setup_inputs(seed: int = 0) -> dict:
    streams_of = jax.random.split(jax.random.key(seed), 4)
    tokens = gaussian_with(streams_of[0], (BATCH, SEQLEN, D), 1.0, 6.0, ((0, 8), (1, 32)), (1, 2, 32, 2.75))
    weights = normal_values(streams_of[1], (D, 3 * E), D ** -0.5, 0.1875)
    dout = normal_values(streams_of[2], (BATCH, SEQLEN, E), 1.0, 6.0, ((0, 8), (1, 32)))
    return {"tokens": tokens, "weights": weights, "dout": dout}


def lowered(array):
    return lax.optimization_barrier(array.astype(jnp.bfloat16)).astype(jnp.float32)

def block_grads(queries, keys, values, grads_out, prefix, suffix, scale):
    hi = lax.Precision.HIGHEST
    count = queries.shape[0]
    position = jnp.arange(count)
    causal = (position[:, None] >= position[None, :])[None]
    score_a = lowered(jnp.where(causal, jnp.einsum('thj,shj->hts', grads_out, values, precision=hi), 0.0))
    score_b = lowered(jnp.where(causal, jnp.einsum('thi,shi->hts', queries, keys, precision=hi), 0.0))
    grad_q = scale * (jnp.einsum('hts,shi->thi', score_a, keys, precision=hi) + jnp.einsum('thj,hij->thi', grads_out, prefix, precision=hi))
    grad_k = scale * jnp.einsum('hts,thi->shi', score_a, queries, precision=hi) + jnp.einsum('shj,hij->shi', values, suffix, precision=hi)
    grad_v = scale * jnp.einsum('hts,thj->shj', score_b, grads_out, precision=hi) + jnp.einsum('shi,hij->shj', keys, suffix, precision=hi)
    return jnp.concatenate([grad_q.reshape(count, -1), grad_k.reshape(count, -1), grad_v.reshape(count, -1)], axis=1)

def reference(tokens, weights, dout):
    hi = lax.Precision.HIGHEST
    inner = HEADS * HD
    block = TOK_DEV
    nblocks = SEQLEN // block
    scale = 1.0 / math.sqrt(HD * SEQLEN)
    factor = 1.0 / math.sqrt(BATCH * SEQLEN)
    flat = tokens.reshape(BATCH * SEQLEN, D)
    proj = jnp.dot(flat, weights, preferred_element_type=jnp.float32).astype(jnp.bfloat16)
    proj = lax.optimization_barrier(proj)
    proj = proj.astype(jnp.float32).reshape(BATCH * nblocks, block, 3, HEADS, HD)
    queries = proj[:, :, 0]
    keys = proj[:, :, 1]
    values = proj[:, :, 2]
    grads_out = dout.astype(jnp.float32).reshape(BATCH * nblocks, block, HEADS, HD)
    kv_local = jnp.einsum('bthi,bthj->bhij', keys, values, precision=hi).reshape(BATCH, nblocks, HEADS, HD, HD)
    qg_local = scale * jnp.einsum('bthi,bthj->bhij', queries, grads_out, precision=hi).reshape(BATCH, nblocks, HEADS, HD, HD)
    prefix = jnp.cumsum(kv_local, axis=1) - kv_local
    suffix = jnp.flip(jnp.cumsum(jnp.flip(qg_local, axis=1), axis=1), axis=1) - qg_local
    prefix = lowered(prefix.reshape(BATCH * nblocks, HEADS, HD, HD))
    suffix = lowered(suffix.reshape(BATCH * nblocks, HEADS, HD, HD))

    def one_block(items):
        return block_grads(items[0], items[1], items[2], items[3], items[4], items[5], scale)
    grads = lax.map(one_block, (queries, keys, values, grads_out, prefix, suffix))
    qkv_grad = grads.reshape(BATCH * SEQLEN, 3 * inner).astype(jnp.bfloat16)
    token_grad = lax.dot_general(qkv_grad, weights, (((1,), (1,)), ((), ())), preferred_element_type=jnp.float32)
    token_grad = token_grad.astype(jnp.bfloat16).reshape(BATCH, SEQLEN, D)
    proj_grad = lax.dot_general(flat, qkv_grad, (((0,), (0,)), ((), ())), preferred_element_type=jnp.float32) * factor
    return (token_grad, proj_grad)
```

```python
import functools
import math

import jax
import jax.numpy as jnp
from jax import lax
from jax.experimental import pallas as pl
from jax.experimental.pallas import tpu as pltpu
from jax.sharding import PartitionSpec as P

MESH = pl.DeviceIdType.MESH
F32 = jnp.float32
BF16 = jnp.bfloat16

HEADS = 8
HD = 128
ROWS = 128
WIDTH = 1024
INNER = HEADS * HD
NX, NY, NZ = 4, 4, 8
CHIPS = NX * NY
FLOWS = 6
FCOLS = 256
GROUPS = 128
STEPS = 7

ORDERS = (
    ("xu", "xv", "yu", "yv", "za", "zb", "zc"),
    ("xv", "xu", "yv", "yu", "zb", "za", "zc"),
    ("yu", "yv", "za", "zb", "xu", "xv", "zc"),
    ("yv", "yu", "zb", "za", "xv", "xu", "zc"),
    ("za", "zb", "xu", "xv", "yu", "yv", "zc"),
    ("zb", "za", "xv", "xu", "yv", "yu", "zc"),
)


def bits_of(x, y, z):
    return {
        "xu": (x % 2 + x // 2) % 2,
        "xv": x // 2,
        "yu": (y % 2 + y // 2) % 2,
        "yv": y // 2,
        "za": (z % 2 + (z // 2) % 2) % 2,
        "zb": (z // 2) % 2,
        "zc": z // 4,
    }


def place_of(flow, bits):
    total = 0
    for step, name in enumerate(ORDERS[flow]):
        total = total + bits[name] * (1 << (STEPS - 1 - step))
    return total


SHIFTS = sorted(
    ((dx, dy) for dx in range(NX) for dy in range(NY) if (dx, dy) != (0, 0)),
    key=lambda d: -(min(d[0], NX - d[0]) + min(d[1], NY - d[1])),
)


def dot(a, b, dims):
    return lax.dot_general(a, b, (dims, ((), ())), preferred_element_type=F32)


def kernel(
    scale,
    factor,
    tok_hbm,
    w_hbm,
    g_hbm,
    tg_ref,
    pg_ref,
    tok,
    g,
    w,
    proj,
    tokf,
    tokp,
    tokt,
    loc,
    s1b,
    tb,
    r1,
    eb,
    r2,
    s3b,
    lpart,
    st,
    qg,
    qf,
    qp,
    acc,
    rb,
    fin,
    finp,
    load_sem,
    pair_send,
    pair_recv,
    p1_send,
    p1_recv,
    p2_send,
    p2_recv,
    qp_send,
    qp_recv,
    rs_send,
    rs_recv,
):
    seq = lax.axis_index("seq")
    z = lax.axis_index("dp")
    core = seq % 2
    chip = seq // 2
    y = chip % NY
    x = chip // NY
    other = 1 - core

    def seq_at(cx, cy):
        return (cx * NY + cy) * 2 + core

    partner = (z, seq + 1 - 2 * core)
    near = {
        "xu": (z, seq_at(x + 1 - 2 * (x % 2), y)),
        "xv": (z, seq_at(3 - x, y)),
        "yu": (z, seq_at(x, y + 1 - 2 * (y % 2))),
        "yv": (z, seq_at(x, 3 - y)),
        "za": (z + 1 - 2 * (z % 2), seq),
        "zb": ((z + 2 * (z % 2) - 1 + NZ) % NZ, seq),
        "zc": ((z + 4) % NZ, seq),
    }
    bits = bits_of(x, y, z)
    targets = []
    for dx, dy in SHIFTS:
        tx, ty = (x + dx) % NX, (y + dy) % NY
        targets.append((tx * NY + ty, (z, seq_at(tx, ty))))

    def remote(src, dst, send, recv, device):
        return pltpu.make_async_remote_copy(
            src_ref=src,
            dst_ref=dst,
            send_sem=send,
            recv_sem=recv,
            device_id=device,
            device_id_type=MESH,
        )

    load_tok = pltpu.make_async_copy(tok_hbm, tok, load_sem.at[0])
    load_g = pltpu.make_async_copy(g_hbm, g, load_sem.at[1])
    load_tok.start()
    load_w = []
    for part in range(3):
        cols = pl.ds(part * INNER, INNER)
        load_w.append(
            pltpu.make_async_copy(w_hbm.at[:, cols], w.at[:, cols], load_sem.at[2 + part])
        )
        load_w[part].start()
    load_g.start()

    barrier = pltpu.get_barrier_semaphore()
    greeted = [partner, near["za"], near["zb"], near["zc"]] + [t[1] for t in targets]
    for device in greeted:
        pl.semaphore_signal(barrier, inc=1, device_id=device, device_id_type=MESH)

    load_tok.wait()
    tokf[...] = tok[...].astype(F32)
    pl.semaphore_wait(barrier, len(greeted))
    send_tok = remote(tokf, tokp, pair_send.at[0], pair_recv.at[0], partner)
    send_tok.start()

    for part in range(3):
        load_w[part].wait()

        def project(i, carry, part=part):
            cols = pl.ds(pl.multiple_of(part * INNER + i * 256, 256), 256)
            proj[:, cols] = dot(tok[...], w[:, cols], ((1,), (0,))).astype(BF16)
            return carry

        lax.fori_loop(0, INNER // 256, project, 0)
    load_g.wait()

    def head_cols(part, h):
        return pl.ds(pl.multiple_of(part * INNER + h * HD, HD), HD)

    def local_state(h, carry):
        q = proj[:, head_cols(0, h)]
        k = proj[:, head_cols(1, h)]
        v = proj[:, head_cols(2, h)]
        d = g[:, head_cols(0, h)]
        kv = dot(k, v, ((0,), (0,)))
        qd = scale * dot(q, d, ((0,), (0,)))
        loc[0, 2 * h] = kv[:64]
        loc[0, 2 * h + 1] = kv[64:]
        loc[1, 2 * h] = qd[:64]
        loc[1, 2 * h + 1] = qd[64:]
        return carry

    lax.fori_loop(0, HEADS, local_state, 0)

    pair_state = remote(loc.at[core], s1b, pair_send.at[1], pair_recv.at[1], partner)
    pair_state.start()

    def own_transpose(i, carry):
        rows = pl.ds(pl.multiple_of(i * 128, 128), 128)
        tokt[rows, 0:128] = tokf[:, rows].T.astype(BF16)
        return carry

    lax.fori_loop(0, WIDTH // 128, own_transpose, 0)

    pair_state.wait_recv()
    tb[...] = loc[other] + s1b[...]
    first = []
    for i, (target, device) in enumerate(targets):
        copy = remote(tb.at[target], r1.at[chip], p1_send.at[i], p1_recv.at[i], device)
        copy.start()
        first.append(copy)
    r1[chip] = tb[chip]

    row = lax.broadcasted_iota(jnp.int32, (ROWS, ROWS), 0)
    col = lax.broadcasted_iota(jnp.int32, (ROWS, ROWS), 1)
    causal = row >= col

    def inside(h, carry):
        q = proj[:, head_cols(0, h)]
        k = proj[:, head_cols(1, h)]
        v = proj[:, head_cols(2, h)]
        d = g[:, head_cols(0, h)]
        sa = jnp.where(causal, dot(d, v, ((1,), (1,))), 0.0).astype(BF16)
        sb = jnp.where(causal, dot(q, k, ((1,), (1,))), 0.0).astype(BF16)
        lpart[:, head_cols(0, h)] = dot(sa, k, ((1,), (0,)))
        lpart[:, head_cols(1, h)] = dot(sa, q, ((0,), (0,)))
        lpart[:, head_cols(2, h)] = dot(sb, d, ((0,), (0,)))
        return carry

    lax.fori_loop(0, HEADS, inside, 0)

    for copy in first:
        copy.wait_recv()

    running = jnp.zeros((64, HD), F32)
    for i in range(CHIPS):
        place = core * i + other * (CHIPS - 1 - i)
        eb[place] = running
        if i < CHIPS - 1:
            running = running + r1[place]
    second = []
    for i, (target, device) in enumerate(targets):
        copy = remote(eb.at[target], r2.at[chip], p2_send.at[i], p2_recv.at[i], device)
        copy.start()
        second.append(copy)
    r2[chip] = eb[chip]

    send_tok.wait_recv()

    def partner_transpose(i, carry):
        rows = pl.ds(pl.multiple_of(i * 128, 128), 128)
        tokt[rows, 128:256] = tokp[:, rows].T.astype(BF16)
        return carry

    lax.fori_loop(0, WIDTH // 128, partner_transpose, 0)

    for copy in second:
        copy.wait_recv()
    pair_scan = remote(r2, s3b, pair_send.at[2], pair_recv.at[2], partner)
    pair_scan.start()
    st[other] = (r2[...] + s1b[...]).astype(BF16)
    pair_scan.wait_recv()
    st[core] = s3b[...].astype(BF16)

    def finish(h):
        q_cols, k_cols, v_cols = (head_cols(part, h) for part in range(3))
        k = proj[:, k_cols]
        v = proj[:, v_cols]
        d = g[:, q_cols]
        prefix = jnp.concatenate([st[0, 2 * h], st[0, 2 * h + 1]], axis=0)
        suffix = jnp.concatenate([st[1, 2 * h], st[1, 2 * h + 1]], axis=0)
        dq = scale * (lpart[:, q_cols] + dot(d, prefix, ((1,), (1,))))
        dk = scale * lpart[:, k_cols] + dot(v, suffix, ((1,), (1,)))
        dv = scale * lpart[:, v_cols] + dot(k, suffix, ((1,), (0,)))
        out = [t.astype(BF16) for t in (dq, dk, dv)]
        for cols, t in zip((q_cols, k_cols, v_cols), out):
            qg[:, cols] = t
        return out

    gather = []
    for pair in range(2):
        for half in range(2):
            out = finish(other * 4 + 2 * pair + half)
            for part in range(3):
                qf[2 * part + pair, :, half * HD : (half + 1) * HD] = out[part].astype(F32)
        for part in range(3):
            flow = 2 * part + pair
            copy = remote(qf.at[flow], qp.at[flow], qp_send.at[flow], qp_recv.at[flow], partner)
            copy.start()
            gather.append((flow, copy))
    for i in range(4):
        finish(core * 4 + i)

    def halving(flow, step, base):
        size = GROUPS >> (step + 1)
        bit = bits[ORDERS[flow][step]]
        return remote(
            acc.at[flow, pl.ds(base + (1 - bit) * size, size)],
            rb.at[flow, pl.ds(size, size)],
            rs_send.at[flow, step],
            rs_recv.at[flow, step],
            near[ORDERS[flow][step]],
        )

    base = [0] * FLOWS
    steps = []
    current = [None] * FLOWS
    for flow, copy in gather:
        copy.wait_recv()
        part, pair = flow // 2, flow % 2
        cols = pl.ds(pl.multiple_of(part * INNER + core * 512 + pair * 256, 256), 256)
        rhs = jnp.concatenate([qg[:, cols], qp[flow].astype(BF16)], axis=0)

        def product(i, carry, flow=flow, rhs=rhs):
            rows = pl.ds(pl.multiple_of(i * 128, 128), 128)
            out = dot(tokt[rows, :], rhs, ((1,), (0,)))
            zero = bits_of(0, 0, i)
            start = place_of(flow, zero)
            for cx in range(NX):
                for cy in range(NY):
                    at = 8 * (cx * NY + cy)
                    acc[flow, start + place_of(flow, bits_of(cx, cy, 0))] = out[at : at + 8]
            return carry

        lax.fori_loop(0, NZ, product, 0)
        current[flow] = halving(flow, 0, 0)
        current[flow].start()
        steps.append(current[flow])

    def token_rows(i, carry):
        rows = pl.ds(pl.multiple_of(i * 256, 256), 256)
        tg_ref[:, rows] = dot(qg[...], w[rows, :], ((1,), (1,))).astype(BF16)
        return carry

    lax.fori_loop(0, WIDTH // 256, token_rows, 0)

    for step in range(STEPS):
        size = GROUPS >> (step + 1)
        for flow, _ in gather:
            current[flow].wait_recv()
            base[flow] = base[flow] + bits[ORDERS[flow][step]] * size
            kept = pl.ds(base[flow], size)
            acc[flow, kept] = acc[flow, kept] + rb[flow, size : 2 * size]
            if step + 1 < STEPS:
                current[flow] = halving(flow, step + 1, base[flow])
                current[flow].start()
                steps.append(current[flow])
            else:
                fin[flow] = acc[flow, base[flow]] * factor

    last = remote(fin, finp, pair_send.at[3], pair_recv.at[3], partner)
    last.start()
    low = core == 0
    for flow in range(FLOWS):
        part, pair = flow // 2, flow % 2
        mine = jnp.where(low, fin[flow, 0:4], fin[flow, 4:8])
        cols = pl.ds(pl.multiple_of(part * INNER + core * 512 + pair * 256, 256), 256)
        pg_ref[:, cols] = mine
    last.wait_recv()
    for flow in range(FLOWS):
        part, pair = flow // 2, flow % 2
        theirs = jnp.where(low, finp[flow, 0:4], finp[flow, 4:8])
        cols = pl.ds(pl.multiple_of(part * INNER + other * 512 + pair * 256, 256), 256)
        pg_ref[:, cols] = theirs

    for copy in [send_tok, pair_state, pair_scan, last] + first + second + steps:
        copy.wait_send()
    for _, copy in gather:
        copy.wait_send()


def shards(tokens, weights, dout):
    rows = tokens.shape[1]
    width = tokens.shape[2]
    seq_count = lax.axis_size("seq")
    data_count = lax.axis_size("dp")
    scale = 1.0 / math.sqrt(HD * rows * seq_count)
    factor = 1.0 / math.sqrt(data_count * rows * seq_count)
    any_space = pl.BlockSpec(memory_space=pl.ANY)
    vmem = pl.BlockSpec(memory_space=pltpu.VMEM)
    slices = (CHIPS, 64, HD)
    dma = pltpu.SemaphoreType.DMA
    token_grad, proj_grad = pl.pallas_call(
        functools.partial(kernel, scale, factor),
        out_shape=(
            jax.ShapeDtypeStruct((rows, width), BF16),
            jax.ShapeDtypeStruct((4, 3 * INNER), F32),
        ),
        in_specs=[any_space] * 3,
        out_specs=(vmem, vmem),
        scratch_shapes=[
            pltpu.VMEM((ROWS, WIDTH), BF16),
            pltpu.VMEM((ROWS, INNER), BF16),
            pltpu.VMEM((WIDTH, 3 * INNER), BF16),
            pltpu.VMEM((ROWS, 3 * INNER), BF16),
            pltpu.VMEM((ROWS, WIDTH), F32),
            pltpu.VMEM((ROWS, WIDTH), F32),
            pltpu.VMEM((WIDTH, 2 * ROWS), BF16),
            pltpu.VMEM((2,) + slices, F32),
            pltpu.VMEM(slices, F32),
            pltpu.VMEM(slices, F32),
            pltpu.VMEM(slices, F32),
            pltpu.VMEM(slices, F32),
            pltpu.VMEM(slices, F32),
            pltpu.VMEM(slices, F32),
            pltpu.VMEM((ROWS, 3 * INNER), F32),
            pltpu.VMEM((2,) + slices, BF16),
            pltpu.VMEM((ROWS, 3 * INNER), BF16),
            pltpu.VMEM((FLOWS, ROWS, FCOLS), F32),
            pltpu.VMEM((FLOWS, ROWS, FCOLS), F32),
            pltpu.VMEM((FLOWS, GROUPS, 8, FCOLS), F32),
            pltpu.VMEM((FLOWS, GROUPS, 8, FCOLS), F32),
            pltpu.VMEM((FLOWS, 8, FCOLS), F32),
            pltpu.VMEM((FLOWS, 8, FCOLS), F32),
            dma((5,)),
            dma((4,)),
            dma((4,)),
            dma((CHIPS - 1,)),
            dma((CHIPS - 1,)),
            dma((CHIPS - 1,)),
            dma((CHIPS - 1,)),
            dma((FLOWS,)),
            dma((FLOWS,)),
            dma((FLOWS, STEPS)),
            dma((FLOWS, STEPS)),
        ],
        compiler_params=pltpu.CompilerParams(
            collective_id=0, has_side_effects=True, vmem_limit_bytes=60 * 1024 * 1024
        ),
    )(tokens.reshape(rows, width), weights, dout.reshape(rows, INNER))
    return (token_grad.reshape(1, rows, width), proj_grad)


def solution(mesh):
    in_specs = (P("dp", "seq", None), P(), P("dp", "seq", None))
    out_specs = (P("dp", "seq", None), P(("dp", "seq"), None))
    return jax.shard_map(shards, mesh=mesh, in_specs=in_specs, out_specs=out_specs, check_vma=False)
```

```python
import functools
import math

import jax
import jax.numpy as jnp
from jax import lax
from jax.experimental import pallas as pl
from jax.experimental.pallas import tpu as pltpu
from jax.sharding import PartitionSpec as P

MESH = pl.DeviceIdType.MESH
F32 = jnp.float32
BF16 = jnp.bfloat16

HEADS = 8
HD = 128
ROWS = 128
WIDTH = 1024
INNER = HEADS * HD
NX, NY, NZ = 4, 4, 8
CHIPS = NX * NY
FLOWS = 6
GROUPS = 128
STEPS = 6

ORDERS = (
    ("xu", "xv", "yu", "yv", "za", "zb", "zc"),
    ("xv", "xu", "yv", "yu", "zb", "za", "zc"),
    ("yu", "yv", "za", "zb", "xu", "xv", "zc"),
    ("yv", "yu", "zb", "za", "xv", "xu", "zc"),
    ("zb", "za", "xv", "xu", "yv", "yu", "zc"),
    ("za", "zb", "xu", "xv", "yu", "yv", "zc"),
)


def bits_of(x, y, z):
    return {
        "xu": (x % 2 + x // 2) % 2,
        "xv": x // 2,
        "yu": (y % 2 + y // 2) % 2,
        "yv": y // 2,
        "za": (z % 2 + (z // 2) % 2) % 2,
        "zb": (z // 2) % 2,
        "zc": z // 4,
    }


def place_of(flow, bits):
    total = bits[ORDERS[flow][0]]
    for step, name in enumerate(ORDERS[flow][1:]):
        total = total + bits[name] * (GROUPS >> (step + 1))
    return total


SHIFTS = sorted(
    ((dx, dy) for dx in range(NX) for dy in range(NY) if (dx, dy) != (0, 0)),
    key=lambda d: -(min(d[0], NX - d[0]) + min(d[1], NY - d[1])),
)


def dot(a, b, dims):
    return lax.dot_general(a, b, (dims, ((), ())), preferred_element_type=F32)


def kernel(
    scale,
    factor,
    tok_hbm,
    w_hbm,
    g_hbm,
    tg_ref,
    pg_ref,
    tok,
    g,
    w,
    proj,
    tokf,
    tkr,
    tkx,
    tokt,
    tokx,
    loc,
    s1b,
    tb,
    r1,
    eb,
    r2,
    s3b,
    lpart,
    st,
    qg,
    qf,
    qr,
    acc,
    rb,
    fin,
    fr,
    load_sem,
    pair_send,
    pair_recv,
    tk_send,
    tk_recv,
    p1_send,
    p1_recv,
    p2_send,
    p2_recv,
    q_send,
    q_recv,
    rs_send,
    rs_recv,
    f_send,
    f_recv,
):
    seq = lax.axis_index("seq")
    z = lax.axis_index("dp")
    core = seq % 2
    chip = seq // 2
    y = chip % NY
    x = chip // NY
    other = 1 - core

    def seq_at(cx, cy):
        return (cx * NY + cy) * 2 + core

    partner = (z, seq + 1 - 2 * core)
    near = {
        "xu": (z, seq_at(x + 1 - 2 * (x % 2), y)),
        "xv": (z, seq_at(3 - x, y)),
        "yu": (z, seq_at(x, y + 1 - 2 * (y % 2))),
        "yv": (z, seq_at(x, 3 - y)),
        "za": (z + 1 - 2 * (z % 2), seq),
        "zb": ((z + 2 * (z % 2) - 1 + NZ) % NZ, seq),
        "zc": ((z + 4) % NZ, seq),
    }
    home = dict(near, zb=((z // 4) * 4 + 3 - z % 4, seq))

    def crossed(device):
        return (device[0], device[1] + 1 - 2 * core)

    bits = bits_of(x, y, z)
    targets = []
    for dx, dy in SHIFTS:
        tx, ty = (x + dx) % NX, (y + dy) % NY
        targets.append((tx * NY + ty, (z, seq_at(tx, ty))))

    def remote(src, dst, send, recv, device):
        return pltpu.make_async_remote_copy(
            src_ref=src,
            dst_ref=dst,
            send_sem=send,
            recv_sem=recv,
            device_id=device,
            device_id_type=MESH,
        )

    load_tok = pltpu.make_async_copy(tok_hbm, tok, load_sem.at[0])
    load_g = pltpu.make_async_copy(g_hbm, g, load_sem.at[1])
    load_tok.start()
    load_w = []
    for part in range(3):
        cols = pl.ds(part * INNER, INNER)
        load_w.append(
            pltpu.make_async_copy(w_hbm.at[:, cols], w.at[:, cols], load_sem.at[2 + part])
        )
        load_w[part].start()
    load_g.start()

    barrier = pltpu.get_barrier_semaphore()
    greeted = [partner, near["za"], near["zb"], near["zc"]] + [t[1] for t in targets]
    greeted += [crossed(near[order[0]]) for order in ORDERS]
    greeted += [home["zb"], crossed(home["zb"])]
    for device in greeted:
        pl.semaphore_signal(barrier, inc=1, device_id=device, device_id_type=MESH)

    load_tok.wait()

    def own_transpose(i, carry):
        rows = pl.ds(pl.multiple_of(i * 128, 128), 128)
        flipped = tok[:, rows].astype(F32).T
        tokf[rows, :] = flipped
        tokt[rows, 0:128] = flipped.astype(BF16)
        return carry

    lax.fori_loop(0, WIDTH // 128, own_transpose, 0)
    pl.semaphore_wait(barrier, len(greeted))
    tokens_out = []
    for flow in range(FLOWS):
        link = near[ORDERS[flow][0]]
        copy = remote(tokf, tkr.at[flow], tk_send.at[flow], tk_recv.at[flow], link)
        copy.start()
        tokens_out.append(copy)
    send_tok = remote(tokf, tkr.at[FLOWS], pair_send.at[0], pair_recv.at[0], partner)
    send_tok.start()

    for part in range(3):
        load_w[part].wait()

        def project(i, carry, part=part):
            cols = pl.ds(pl.multiple_of(part * INNER + i * 256, 256), 256)
            proj[:, cols] = dot(tok[...], w[:, cols], ((1,), (0,))).astype(BF16)
            return carry

        lax.fori_loop(0, INNER // 256, project, 0)
    load_g.wait()

    def head_cols(part, h):
        return pl.ds(pl.multiple_of(part * INNER + h * HD, HD), HD)

    def local_state(h, carry):
        q = proj[:, head_cols(0, h)]
        k = proj[:, head_cols(1, h)]
        v = proj[:, head_cols(2, h)]
        d = g[:, head_cols(0, h)]
        kv = dot(k, v, ((0,), (0,)))
        qd = scale * dot(q, d, ((0,), (0,)))
        loc[0, 2 * h] = kv[:64]
        loc[0, 2 * h + 1] = kv[64:]
        loc[1, 2 * h] = qd[:64]
        loc[1, 2 * h + 1] = qd[64:]
        return carry

    lax.fori_loop(0, HEADS, local_state, 0)

    pair_state = remote(loc.at[core], s1b, pair_send.at[1], pair_recv.at[1], partner)
    pair_state.start()

    pair_state.wait_recv()
    tb[...] = loc[other] + s1b[...]
    first = []
    for i, (target, device) in enumerate(targets):
        copy = remote(tb.at[target], r1.at[chip], p1_send.at[i], p1_recv.at[i], device)
        copy.start()
        first.append(copy)
    r1[chip] = tb[chip]

    row = lax.broadcasted_iota(jnp.int32, (ROWS, ROWS), 0)
    col = lax.broadcasted_iota(jnp.int32, (ROWS, ROWS), 1)
    causal = row >= col

    def inside(h, carry):
        q = proj[:, head_cols(0, h)]
        k = proj[:, head_cols(1, h)]
        v = proj[:, head_cols(2, h)]
        d = g[:, head_cols(0, h)]
        sa = jnp.where(causal, dot(d, v, ((1,), (1,))), 0.0).astype(BF16)
        sb = jnp.where(causal, dot(q, k, ((1,), (1,))), 0.0).astype(BF16)
        lpart[:, head_cols(0, h)] = dot(sa, k, ((1,), (0,)))
        lpart[:, head_cols(1, h)] = dot(sa, q, ((0,), (0,)))
        lpart[:, head_cols(2, h)] = dot(sb, d, ((0,), (0,)))
        return carry

    lax.fori_loop(0, HEADS, inside, 0)

    relays = []
    for flow in range(FLOWS):
        tokens_out[flow].wait_recv()
        copy = remote(
            tkr.at[flow], tkx.at[flow], tk_send.at[FLOWS + flow], tk_recv.at[FLOWS + flow], partner
        )
        copy.start()
        relays.append(copy)

    for copy in first:
        copy.wait_recv()

    running = jnp.zeros((64, HD), F32)
    for i in range(CHIPS):
        place = core * i + other * (CHIPS - 1 - i)
        eb[place] = running
        if i < CHIPS - 1:
            running = running + r1[place]
    second = []
    for i, (target, device) in enumerate(targets):
        copy = remote(eb.at[target], r2.at[chip], p2_send.at[i], p2_recv.at[i], device)
        copy.start()
        second.append(copy)
    r2[chip] = eb[chip]

    send_tok.wait_recv()
    tokt[:, 128:256] = tkr[FLOWS].astype(BF16)
    for flow in range(FLOWS):
        tokx[flow, :, 0:128] = tkr[flow].astype(BF16)
        relays[flow].wait_recv()
        tokx[flow, :, 128:256] = tkx[flow].astype(BF16)

    for copy in second:
        copy.wait_recv()
    pair_scan = remote(r2, s3b, pair_send.at[2], pair_recv.at[2], partner)
    pair_scan.start()
    st[other] = (r2[...] + s1b[...]).astype(BF16)
    pair_scan.wait_recv()
    st[core] = s3b[...].astype(BF16)

    def finish(h):
        q_cols, k_cols, v_cols = (head_cols(part, h) for part in range(3))
        k = proj[:, k_cols]
        v = proj[:, v_cols]
        d = g[:, q_cols]
        prefix = jnp.concatenate([st[0, 2 * h], st[0, 2 * h + 1]], axis=0)
        suffix = jnp.concatenate([st[1, 2 * h], st[1, 2 * h + 1]], axis=0)
        dq = scale * (lpart[:, q_cols] + dot(d, prefix, ((1,), (1,))))
        dk = scale * lpart[:, k_cols] + dot(v, suffix, ((1,), (1,)))
        dv = scale * lpart[:, v_cols] + dot(k, suffix, ((1,), (0,)))
        out = [t.astype(BF16) for t in (dq, dk, dv)]
        for part, (cols, t) in enumerate(zip((q_cols, k_cols, v_cols), out)):
            qg[:, cols] = t
            qf[part, h] = t.astype(F32)

    first_bit = [bits[ORDERS[flow][0]] for flow in range(FLOWS)]

    def head_of(flow, at_core, bit):
        return 4 * at_core + 2 * (flow % 2) + bit

    gather = [None] * FLOWS
    for pair in range(2):
        for h in (0, 1, 4, 5):
            finish(2 * pair + h)
        for part in (2, 1, 0):
            flow = 2 * part + pair
            bit = first_bit[flow]
            link = ORDERS[flow][0]
            copies = []
            for i, (at_core, at_bit, device) in enumerate(
                (
                    (core, 1 - bit, near[link]),
                    (other, 1 - bit, crossed(near[link])),
                    (other, bit, partner),
                )
            ):
                copy = remote(
                    qf.at[part, head_of(flow, at_core, at_bit)],
                    qr.at[flow, i],
                    q_send.at[flow, i],
                    q_recv.at[flow, i],
                    device,
                )
                copy.start()
                copies.append(copy)
            gather[flow] = copies

    for part in range(3):
        blocks = []
        for pair in range(2):
            flow = 2 * part + pair
            gather[flow][2].wait_recv()
            own = qg[:, head_cols(part, head_of(flow, core, first_bit[flow]))]
            blocks.append(jnp.concatenate([own, qr[flow, 2].astype(BF16)], axis=0))
        rhs = jnp.concatenate(blocks, axis=1)

        def chip_product(i, carry, part=part, rhs=rhs):
            rows = pl.ds(pl.multiple_of(i * 128, 128), 128)
            out = dot(tokt[rows, :], rhs, ((1,), (0,)))
            for pair in range(2):
                flow = 2 * part + pair
                start = place_of(flow, bits_of(0, 0, i))
                for cx in range(NX):
                    for cy in range(NY):
                        at = 8 * (cx * NY + cy)
                        block = out[at : at + 8, pair * 128 : pair * 128 + 128]
                        acc[flow, start + place_of(flow, bits_of(cx, cy, 0))] = block
            return carry

        lax.fori_loop(0, NZ, chip_product, 0)

    def halving(flow, step, base):
        size = GROUPS >> (step + 1)
        name = ORDERS[flow][step + 1]
        return remote(
            acc.at[flow, pl.ds(base + (1 - bits[name]) * size, size)],
            rb.at[flow, pl.ds(size, size)],
            rs_send.at[flow, step],
            rs_recv.at[flow, step],
            near[name],
        )

    base = [0] * FLOWS
    steps = []
    current = [None] * FLOWS
    flow_order = (4, 2, 0, 5, 3, 1)
    for flow in flow_order:
        gather[flow][0].wait_recv()
        gather[flow][1].wait_recv()
        rhs = jnp.concatenate([qr[flow, 0].astype(BF16), qr[flow, 1].astype(BF16)], axis=0)

        def product(i, carry, flow=flow, rhs=rhs):
            rows = pl.ds(pl.multiple_of(i * 128, 128), 128)
            out = dot(tokx[flow, rows, :], rhs, ((1,), (0,)))
            start = place_of(flow, bits_of(0, 0, i))
            for cx in range(NX):
                for cy in range(NY):
                    at = 8 * (cx * NY + cy)
                    place = start + place_of(flow, bits_of(cx, cy, 0))
                    acc[flow, place] = acc[flow, place] + out[at : at + 8]
            return carry

        lax.fori_loop(0, NZ, product, 0)
        current[flow] = halving(flow, 0, 0)
        current[flow].start()
        steps.append(current[flow])

    def token_rows(i, carry):
        rows = pl.ds(pl.multiple_of(i * 256, 256), 256)
        tg_ref[:, rows] = dot(qg[...], w[rows, :], ((1,), (1,))).astype(BF16)
        return carry

    lax.fori_loop(0, WIDTH // 256, token_rows, 0)

    def hand_out(flow):
        bit = first_bit[flow]
        device = home[ORDERS[flow][0]]
        fin[flow, 0] = acc[flow, base[flow] + bit] * factor
        fin[flow, 1] = acc[flow, base[flow] + 1 - bit] * factor
        copies = []
        for i, (src, to) in enumerate(((1, device), (1, crossed(device)), (0, partner))):
            copy = remote(
                fin.at[flow, src], fr.at[flow, i], f_send.at[flow, i], f_recv.at[flow, i], to
            )
            copy.start()
            copies.append(copy)
        return copies

    handed = [None] * FLOWS
    for step in range(STEPS):
        size = GROUPS >> (step + 1)
        for flow in flow_order:
            current[flow].wait_recv()
            base[flow] = base[flow] + bits[ORDERS[flow][step + 1]] * size
            kept = pl.ds(base[flow], size)
            acc[flow, kept] = acc[flow, kept] + rb[flow, size : 2 * size]
            if step + 1 < STEPS:
                current[flow] = halving(flow, step + 1, base[flow])
                current[flow].start()
                steps.append(current[flow])
            else:
                handed[flow] = hand_out(flow)

    low = core == 0

    def put(flow, at_core, bit, rows):
        cols = head_cols(flow // 2, head_of(flow, at_core, bit))
        pg_ref[:, cols] = jnp.where(low, rows[0:4], rows[4:8])

    for flow in flow_order:
        put(flow, core, first_bit[flow], fin[flow, 0])
    for flow in flow_order:
        bit = first_bit[flow]
        for copy in handed[flow]:
            copy.wait_recv()
        put(flow, core, 1 - bit, fr[flow, 0])
        put(flow, other, 1 - bit, fr[flow, 1])
        put(flow, other, bit, fr[flow, 2])

    for copy in [send_tok, pair_state, pair_scan] + tokens_out + relays + first + second + steps:
        copy.wait_send()
    for flow in range(FLOWS):
        for copy in gather[flow] + handed[flow]:
            copy.wait_send()


def shards(tokens, weights, dout):
    rows = tokens.shape[1]
    width = tokens.shape[2]
    seq_count = lax.axis_size("seq")
    data_count = lax.axis_size("dp")
    scale = 1.0 / math.sqrt(HD * rows * seq_count)
    factor = 1.0 / math.sqrt(data_count * rows * seq_count)
    any_space = pl.BlockSpec(memory_space=pl.ANY)
    vmem = pl.BlockSpec(memory_space=pltpu.VMEM)
    slices = (CHIPS, 64, HD)
    dma = pltpu.SemaphoreType.DMA
    token_grad, proj_grad = pl.pallas_call(
        functools.partial(kernel, scale, factor),
        out_shape=(
            jax.ShapeDtypeStruct((rows, width), BF16),
            jax.ShapeDtypeStruct((4, 3 * INNER), F32),
        ),
        in_specs=[any_space] * 3,
        out_specs=(vmem, vmem),
        scratch_shapes=[
            pltpu.VMEM((ROWS, WIDTH), BF16),
            pltpu.VMEM((ROWS, INNER), BF16),
            pltpu.VMEM((WIDTH, 3 * INNER), BF16),
            pltpu.VMEM((ROWS, 3 * INNER), BF16),
            pltpu.VMEM((WIDTH, ROWS), F32),
            pltpu.VMEM((FLOWS + 1, WIDTH, ROWS), F32),
            pltpu.VMEM((FLOWS, WIDTH, ROWS), F32),
            pltpu.VMEM((WIDTH, 2 * ROWS), BF16),
            pltpu.VMEM((FLOWS, WIDTH, 2 * ROWS), BF16),
            pltpu.VMEM((2,) + slices, F32),
            pltpu.VMEM(slices, F32),
            pltpu.VMEM(slices, F32),
            pltpu.VMEM(slices, F32),
            pltpu.VMEM(slices, F32),
            pltpu.VMEM(slices, F32),
            pltpu.VMEM(slices, F32),
            pltpu.VMEM((ROWS, 3 * INNER), F32),
            pltpu.VMEM((2,) + slices, BF16),
            pltpu.VMEM((ROWS, 3 * INNER), BF16),
            pltpu.VMEM((3, HEADS, ROWS, HD), F32),
            pltpu.VMEM((FLOWS, 3, ROWS, HD), F32),
            pltpu.VMEM((FLOWS, GROUPS, 8, HD), F32),
            pltpu.VMEM((FLOWS, GROUPS, 8, HD), F32),
            pltpu.VMEM((FLOWS, 2, 8, HD), F32),
            pltpu.VMEM((FLOWS, 3, 8, HD), F32),
            dma((5,)),
            dma((3,)),
            dma((3,)),
            dma((2 * FLOWS,)),
            dma((2 * FLOWS,)),
            dma((CHIPS - 1,)),
            dma((CHIPS - 1,)),
            dma((CHIPS - 1,)),
            dma((CHIPS - 1,)),
            dma((FLOWS, 3)),
            dma((FLOWS, 3)),
            dma((FLOWS, STEPS)),
            dma((FLOWS, STEPS)),
            dma((FLOWS, 3)),
            dma((FLOWS, 3)),
        ],
        compiler_params=pltpu.CompilerParams(
            collective_id=0, has_side_effects=True, vmem_limit_bytes=60 * 1024 * 1024
        ),
    )(tokens.reshape(rows, width), weights, dout.reshape(rows, INNER))
    return (token_grad.reshape(1, rows, width), proj_grad)


def solution(mesh):
    in_specs = (P("dp", "seq", None), P(), P("dp", "seq", None))
    out_specs = (P("dp", "seq", None), P(("dp", "seq"), None))
    return jax.shard_map(shards, mesh=mesh, in_specs=in_specs, out_specs=out_specs, check_vma=False)
```

```python
import functools
import math

import jax
import jax.numpy as jnp
from jax import lax
from jax.experimental import pallas as pl
from jax.experimental.pallas import tpu as pltpu
from jax.sharding import PartitionSpec as P

MESH = pl.DeviceIdType.MESH
F32 = jnp.float32
BF16 = jnp.bfloat16

HEADS = 8
HD = 128
ROWS = 128
WIDTH = 1024
INNER = HEADS * HD
NX, NY, NZ = 4, 4, 8
CHIPS = NX * NY
CHUNKS = 2
SLICE = 32
FLOWS = 6
GROUPS = 128
STEPS = 6

ORDERS = (
    ("xu", "xv", "yu", "yv", "za", "zb", "zc"),
    ("xv", "xu", "yv", "yu", "zb", "za", "zc"),
    ("yu", "yv", "za", "zb", "xu", "xv", "zc"),
    ("yv", "yu", "zb", "za", "xv", "xu", "zc"),
    ("zb", "za", "xv", "xu", "yv", "yu", "zc"),
    ("za", "zb", "xu", "xv", "yu", "yv", "zc"),
)


def bits_of(x, y, z):
    return {
        "xu": (x % 2 + x // 2) % 2,
        "xv": x // 2,
        "yu": (y % 2 + y // 2) % 2,
        "yv": y // 2,
        "za": (z % 2 + (z // 2) % 2) % 2,
        "zb": (z // 2) % 2,
        "zc": z // 4,
    }


def place_of(flow, bits):
    total = bits[ORDERS[flow][0]]
    for step, name in enumerate(ORDERS[flow][1:]):
        total = total + bits[name] * (GROUPS >> (step + 1))
    return total


SHIFTS = sorted(
    ((dx, dy) for dx in range(NX) for dy in range(NY) if (dx, dy) != (0, 0)),
    key=lambda d: -(min(d[0], NX - d[0]) + min(d[1], NY - d[1])),
)


def dot(a, b, dims):
    return lax.dot_general(a, b, (dims, ((), ())), preferred_element_type=F32)


def kernel(
    scale,
    factor,
    tok_hbm,
    w_hbm,
    g_hbm,
    tg_ref,
    pg_ref,
    tok,
    g,
    w,
    proj,
    tokf,
    tkr,
    tkx,
    tokt,
    loc,
    s1b,
    tb,
    r1,
    eb,
    r2,
    s3b,
    lpart,
    st,
    qg,
    qf,
    qr,
    acc,
    rb,
    fin,
    fr,
    load_sem,
    pair_send,
    pair_recv,
    tk_send,
    tk_recv,
    p1_send,
    p1_recv,
    p2_send,
    p2_recv,
    q_send,
    q_recv,
    rs_send,
    rs_recv,
    f_send,
    f_recv,
):
    seq = lax.axis_index("seq")
    z = lax.axis_index("dp")
    core = seq % 2
    chip = seq // 2
    y = chip % NY
    x = chip // NY
    other = 1 - core

    def seq_at(cx, cy):
        return (cx * NY + cy) * 2 + core

    partner = (z, seq + 1 - 2 * core)
    near = {
        "xu": (z, seq_at(x + 1 - 2 * (x % 2), y)),
        "xv": (z, seq_at(3 - x, y)),
        "yu": (z, seq_at(x, y + 1 - 2 * (y % 2))),
        "yv": (z, seq_at(x, 3 - y)),
        "za": (z + 1 - 2 * (z % 2), seq),
        "zb": ((z + 2 * (z % 2) - 1 + NZ) % NZ, seq),
        "zc": ((z + 4) % NZ, seq),
    }
    home = dict(near, zb=((z // 4) * 4 + 3 - z % 4, seq))

    def crossed(device):
        return (device[0], device[1] + 1 - 2 * core)

    bits = bits_of(x, y, z)
    targets = []
    for dx, dy in SHIFTS:
        tx, ty = (x + dx) % NX, (y + dy) % NY
        targets.append((tx * NY + ty, (z, seq_at(tx, ty))))

    def remote(src, dst, send, recv, device):
        return pltpu.make_async_remote_copy(
            src_ref=src,
            dst_ref=dst,
            send_sem=send,
            recv_sem=recv,
            device_id=device,
            device_id_type=MESH,
        )

    load_tok = pltpu.make_async_copy(tok_hbm, tok, load_sem.at[0])
    load_g = pltpu.make_async_copy(g_hbm, g, load_sem.at[1])
    load_tok.start()
    load_w = []
    for part in range(3):
        cols = pl.ds(part * INNER, INNER)
        load_w.append(
            pltpu.make_async_copy(w_hbm.at[:, cols], w.at[:, cols], load_sem.at[2 + part])
        )
        load_w[part].start()
    load_g.start()

    barrier = pltpu.get_barrier_semaphore()
    greeted = [partner, near["za"], near["zb"], near["zc"]] + [t[1] for t in targets]
    greeted += [crossed(near[order[0]]) for order in ORDERS]
    greeted += [home["zb"], crossed(home["zb"])]
    for device in greeted:
        pl.semaphore_signal(barrier, inc=1, device_id=device, device_id_type=MESH)

    load_tok.wait()

    def own_transpose(i, carry):
        rows = pl.ds(pl.multiple_of(i * 128, 128), 128)
        flipped = tok[:, rows].astype(F32).T
        tokf[rows, :] = flipped
        tokt[rows, 0:128] = flipped.astype(BF16)
        return carry

    lax.fori_loop(0, WIDTH // 128, own_transpose, 0)

    for part in range(3):
        load_w[part].wait()

        def project(i, carry, part=part):
            cols = pl.ds(pl.multiple_of(part * INNER + i * 256, 256), 256)
            proj[:, cols] = dot(tok[...], w[:, cols], ((1,), (0,))).astype(BF16)
            return carry

        lax.fori_loop(0, INNER // 256, project, 0)
    load_g.wait()

    def head_cols(part, h):
        return pl.ds(pl.multiple_of(part * INNER + h * HD, HD), HD)

    pl.semaphore_wait(barrier, len(greeted))
    half = WIDTH // 2
    tokens_out = {}
    relays = {}

    def send_tokens(flows, part):
        rows = pl.ds(part * half, half)
        for flow in flows:
            copy = remote(
                tokf.at[rows],
                tkr.at[flow, rows],
                tk_send.at[flow, part],
                tk_recv.at[flow, part],
                near[ORDERS[flow][0]],
            )
            copy.start()
            tokens_out[flow, part] = copy

    def relay_tokens(flows, part):
        rows = pl.ds(part * half, half)
        for flow in flows:
            tokens_out[flow, part].wait_recv()
            copy = remote(
                tkr.at[flow, rows],
                tkx.at[flow, rows],
                tk_send.at[FLOWS + flow, part],
                tk_recv.at[FLOWS + flow, part],
                partner,
            )
            copy.start()
            relays[flow, part] = copy

    z_flows, xy_flows = (4, 5), (0, 1, 2, 3)
    send_tokens(z_flows, 0)
    send_tokens(z_flows, 1)

    pair_state = []
    for chunk in range(CHUNKS):

        def local_state(i, carry, chunk=chunk):
            h = 4 * chunk + i
            q = proj[:, head_cols(0, h)]
            k = proj[:, head_cols(1, h)]
            v = proj[:, head_cols(2, h)]
            d = g[:, head_cols(0, h)]
            loc[0, chunk, pl.ds(4 * i, 4)] = dot(k, v, ((0,), (0,))).reshape(4, SLICE, HD)
            loc[1, chunk, pl.ds(4 * i, 4)] = (scale * dot(q, d, ((0,), (0,)))).reshape(4, SLICE, HD)
            return carry

        lax.fori_loop(0, HEADS // CHUNKS, local_state, 0)
        copy = remote(
            loc.at[core, chunk],
            s1b.at[chunk],
            pair_send.at[chunk],
            pair_recv.at[chunk],
            partner,
        )
        copy.start()
        pair_state.append(copy)

    first = []
    for chunk in range(CHUNKS):
        pair_state[chunk].wait_recv()
        tb[chunk] = loc[other, chunk] + s1b[chunk]
        copies = []
        for i, (target, device) in enumerate(targets):
            copy = remote(
                tb.at[chunk, target],
                r1.at[chunk, chip],
                p1_send.at[chunk, i],
                p1_recv.at[chunk, i],
                device,
            )
            copy.start()
            copies.append(copy)
        first.append(copies)
        r1[chunk, chip] = tb[chunk, chip]
    send_tokens(xy_flows, 0)
    send_tok = remote(tokf, tkr.at[FLOWS], pair_send.at[4], pair_recv.at[4], partner)
    send_tok.start()

    row = lax.broadcasted_iota(jnp.int32, (ROWS, ROWS), 0)
    col = lax.broadcasted_iota(jnp.int32, (ROWS, ROWS), 1)
    causal = row >= col

    def inside(h, carry):
        q = proj[:, head_cols(0, h)]
        k = proj[:, head_cols(1, h)]
        v = proj[:, head_cols(2, h)]
        d = g[:, head_cols(0, h)]
        sa = jnp.where(causal, dot(d, v, ((1,), (1,))), 0.0).astype(BF16)
        sb = jnp.where(causal, dot(q, k, ((1,), (1,))), 0.0).astype(BF16)
        lpart[:, head_cols(0, h)] = dot(sa, k, ((1,), (0,)))
        lpart[:, head_cols(1, h)] = dot(sa, q, ((0,), (0,)))
        lpart[:, head_cols(2, h)] = dot(sb, d, ((0,), (0,)))
        return carry

    lax.fori_loop(0, HEADS, inside, 0)

    second = []
    for chunk in range(CHUNKS):
        for copy in first[chunk]:
            copy.wait_recv()
        running = jnp.zeros((SLICE, HD), F32)
        for i in range(CHIPS):
            place = core * i + other * (CHIPS - 1 - i)
            eb[chunk, place] = running
            if i < CHIPS - 1:
                running = running + r1[chunk, place]
        copies = []
        for i, (target, device) in enumerate(targets):
            copy = remote(
                eb.at[chunk, target],
                r2.at[chunk, chip],
                p2_send.at[chunk, i],
                p2_recv.at[chunk, i],
                device,
            )
            copy.start()
            copies.append(copy)
        second.append(copies)
        r2[chunk, chip] = eb[chunk, chip]

    send_tokens(xy_flows, 1)
    relay_tokens(z_flows, 0)
    relay_tokens(z_flows, 1)
    relay_tokens(xy_flows, 0)
    send_tok.wait_recv()
    tokt[:, 128:256] = tkr[FLOWS].astype(BF16)

    pair_scan = []
    for chunk in range(CHUNKS):
        for copy in second[chunk]:
            copy.wait_recv()
        copy = remote(
            r2.at[chunk],
            s3b.at[chunk],
            pair_send.at[2 + chunk],
            pair_recv.at[2 + chunk],
            partner,
        )
        copy.start()
        pair_scan.append(copy)
        st[other, chunk] = (r2[chunk] + s1b[chunk]).astype(BF16)

    def finish(h):
        q_cols, k_cols, v_cols = (head_cols(part, h) for part in range(3))
        k = proj[:, k_cols]
        v = proj[:, v_cols]
        d = g[:, q_cols]
        at = 4 * (h % 4)
        prefix = st[0, h // 4, at : at + 4].reshape(HD, HD)
        suffix = st[1, h // 4, at : at + 4].reshape(HD, HD)
        dq = scale * (lpart[:, q_cols] + dot(d, prefix, ((1,), (1,))))
        dk = scale * lpart[:, k_cols] + dot(v, suffix, ((1,), (1,)))
        dv = scale * lpart[:, v_cols] + dot(k, suffix, ((1,), (0,)))
        out = [t.astype(BF16) for t in (dq, dk, dv)]
        for part, (cols, t) in enumerate(zip((q_cols, k_cols, v_cols), out)):
            qg[:, cols] = t
            qf[part, h] = t.astype(F32)

    first_bit = [bits[ORDERS[flow][0]] for flow in range(FLOWS)]

    def head_of(flow, at_core, bit):
        return 4 * (flow % 2) + 2 * at_core + bit

    gather = [None] * FLOWS
    for pair in range(2):
        pair_scan[pair].wait_recv()
        st[core, pair] = s3b[pair].astype(BF16)
        for h in range(4):
            finish(4 * pair + h)
        for part in (2, 1, 0):
            flow = 2 * part + pair
            bit = first_bit[flow]
            link = ORDERS[flow][0]
            copies = []
            for i, (at_core, at_bit, device) in enumerate(
                (
                    (core, 1 - bit, near[link]),
                    (other, 1 - bit, crossed(near[link])),
                    (other, bit, partner),
                )
            ):
                copy = remote(
                    qf.at[part, head_of(flow, at_core, at_bit)],
                    qr.at[flow, i],
                    q_send.at[flow, i],
                    q_recv.at[flow, i],
                    device,
                )
                copy.start()
                copies.append(copy)
            gather[flow] = copies

    relay_tokens(xy_flows, 1)

    def chip_part(pair):
        blocks = []
        for part in range(3):
            flow = 2 * part + pair
            gather[flow][2].wait_recv()
            own = qg[:, head_cols(part, head_of(flow, core, first_bit[flow]))]
            blocks.append(jnp.concatenate([own, qr[flow, 2].astype(BF16)], axis=0))
        rhs = jnp.concatenate(blocks, axis=1)

        def chip_product(i, carry):
            rows = pl.ds(pl.multiple_of(i * 128, 128), 128)
            out = dot(tokt[rows, :], rhs, ((1,), (0,)))
            for part in range(3):
                flow = 2 * part + pair
                start = place_of(flow, bits_of(0, 0, i))
                for cx in range(NX):
                    for cy in range(NY):
                        at = 8 * (cx * NY + cy)
                        block = out[at : at + 8, part * 128 : part * 128 + 128]
                        acc[flow, start + place_of(flow, bits_of(cx, cy, 0))] = block
            return carry

        lax.fori_loop(0, NZ, chip_product, 0)

    def halving(flow, step, base):
        size = GROUPS >> (step + 1)
        name = ORDERS[flow][step + 1]
        return remote(
            acc.at[flow, pl.ds(base + (1 - bits[name]) * size, size)],
            rb.at[flow, pl.ds(size, size)],
            rs_send.at[flow, step],
            rs_recv.at[flow, step],
            near[name],
        )

    base = [0] * FLOWS
    steps = []
    current = [None] * FLOWS
    flow_order = (4, 2, 0, 5, 3, 1)
    for flow in flow_order:
        if flow in (4, 5):
            chip_part(flow % 2)
        relays[flow, 0].wait_recv()
        relays[flow, 1].wait_recv()
        gather[flow][0].wait_recv()
        gather[flow][1].wait_recv()
        rhs = jnp.concatenate([qr[flow, 0].astype(BF16), qr[flow, 1].astype(BF16)], axis=0)

        def product(i, carry, flow=flow, rhs=rhs):
            rows = pl.ds(pl.multiple_of(i * 128, 128), 128)
            lhs = jnp.concatenate(
                [tkr[flow, rows, :].astype(BF16), tkx[flow, rows, :].astype(BF16)], axis=1
            )
            out = dot(lhs, rhs, ((1,), (0,)))
            start = place_of(flow, bits_of(0, 0, i))
            for cx in range(NX):
                for cy in range(NY):
                    at = 8 * (cx * NY + cy)
                    place = start + place_of(flow, bits_of(cx, cy, 0))
                    acc[flow, place] = acc[flow, place] + out[at : at + 8]
            return carry

        lax.fori_loop(0, NZ, product, 0)
        current[flow] = halving(flow, 0, 0)
        current[flow].start()
        steps.append(current[flow])

    def token_rows(i, carry):
        rows = pl.ds(pl.multiple_of(i * 256, 256), 256)
        tg_ref[:, rows] = dot(qg[...], w[rows, :], ((1,), (1,))).astype(BF16)
        return carry

    lax.fori_loop(0, WIDTH // 256, token_rows, 0)

    def hand_out(flow):
        bit = first_bit[flow]
        device = home[ORDERS[flow][0]]
        fin[flow, 0] = acc[flow, base[flow] + bit] * factor
        fin[flow, 1] = acc[flow, base[flow] + 1 - bit] * factor
        copies = []
        for i, (src, to) in enumerate(((1, device), (1, crossed(device)), (0, partner))):
            copy = remote(
                fin.at[flow, src], fr.at[flow, i], f_send.at[flow, i], f_recv.at[flow, i], to
            )
            copy.start()
            copies.append(copy)
        return copies

    handed = [None] * FLOWS
    for step in range(STEPS):
        size = GROUPS >> (step + 1)
        for flow in flow_order:
            current[flow].wait_recv()
            base[flow] = base[flow] + bits[ORDERS[flow][step + 1]] * size
            kept = pl.ds(base[flow], size)
            acc[flow, kept] = acc[flow, kept] + rb[flow, size : 2 * size]
            if step + 1 < STEPS:
                current[flow] = halving(flow, step + 1, base[flow])
                current[flow].start()
                steps.append(current[flow])
            else:
                handed[flow] = hand_out(flow)

    low = core == 0

    def put(flow, at_core, bit, rows):
        cols = head_cols(flow // 2, head_of(flow, at_core, bit))
        pg_ref[:, cols] = jnp.where(low, rows[0:4], rows[4:8])

    for flow in flow_order:
        put(flow, core, first_bit[flow], fin[flow, 0])
    for flow in flow_order:
        bit = first_bit[flow]
        for copy in handed[flow]:
            copy.wait_recv()
        put(flow, core, 1 - bit, fr[flow, 0])
        put(flow, other, 1 - bit, fr[flow, 1])
        put(flow, other, bit, fr[flow, 2])

    for copy in [send_tok] + pair_state + pair_scan + steps:
        copy.wait_send()
    for copies in [tokens_out.values(), relays.values()] + first + second:
        for copy in copies:
            copy.wait_send()
    for flow in range(FLOWS):
        for copy in gather[flow] + handed[flow]:
            copy.wait_send()


def shards(tokens, weights, dout):
    rows = tokens.shape[1]
    width = tokens.shape[2]
    seq_count = lax.axis_size("seq")
    data_count = lax.axis_size("dp")
    scale = 1.0 / math.sqrt(HD * rows * seq_count)
    factor = 1.0 / math.sqrt(data_count * rows * seq_count)
    any_space = pl.BlockSpec(memory_space=pl.ANY)
    vmem = pl.BlockSpec(memory_space=pltpu.VMEM)
    slices = (CHUNKS, CHIPS, SLICE, HD)
    dma = pltpu.SemaphoreType.DMA
    token_grad, proj_grad = pl.pallas_call(
        functools.partial(kernel, scale, factor),
        out_shape=(
            jax.ShapeDtypeStruct((rows, width), BF16),
            jax.ShapeDtypeStruct((4, 3 * INNER), F32),
        ),
        in_specs=[any_space] * 3,
        out_specs=(vmem, vmem),
        scratch_shapes=[
            pltpu.VMEM((ROWS, WIDTH), BF16),
            pltpu.VMEM((ROWS, INNER), BF16),
            pltpu.VMEM((WIDTH, 3 * INNER), BF16),
            pltpu.VMEM((ROWS, 3 * INNER), BF16),
            pltpu.VMEM((WIDTH, ROWS), F32),
            pltpu.VMEM((FLOWS + 1, WIDTH, ROWS), F32),
            pltpu.VMEM((FLOWS, WIDTH, ROWS), F32),
            pltpu.VMEM((WIDTH, 2 * ROWS), BF16),
            pltpu.VMEM((2,) + slices, F32),
            pltpu.VMEM(slices, F32),
            pltpu.VMEM(slices, F32),
            pltpu.VMEM(slices, F32),
            pltpu.VMEM(slices, F32),
            pltpu.VMEM(slices, F32),
            pltpu.VMEM(slices, F32),
            pltpu.VMEM((ROWS, 3 * INNER), F32),
            pltpu.VMEM((2,) + slices, BF16),
            pltpu.VMEM((ROWS, 3 * INNER), BF16),
            pltpu.VMEM((3, HEADS, ROWS, HD), F32),
            pltpu.VMEM((FLOWS, 3, ROWS, HD), F32),
            pltpu.VMEM((FLOWS, GROUPS, 8, HD), F32),
            pltpu.VMEM((FLOWS, GROUPS, 8, HD), F32),
            pltpu.VMEM((FLOWS, 2, 8, HD), F32),
            pltpu.VMEM((FLOWS, 3, 8, HD), F32),
            dma((5,)),
            dma((5,)),
            dma((5,)),
            dma((2 * FLOWS, 2)),
            dma((2 * FLOWS, 2)),
            dma((CHUNKS, CHIPS - 1)),
            dma((CHUNKS, CHIPS - 1)),
            dma((CHUNKS, CHIPS - 1)),
            dma((CHUNKS, CHIPS - 1)),
            dma((FLOWS, 3)),
            dma((FLOWS, 3)),
            dma((FLOWS, STEPS)),
            dma((FLOWS, STEPS)),
            dma((FLOWS, 3)),
            dma((FLOWS, 3)),
        ],
        compiler_params=pltpu.CompilerParams(
            collective_id=0, has_side_effects=True, vmem_limit_bytes=60 * 1024 * 1024
        ),
    )(tokens.reshape(rows, width), weights, dout.reshape(rows, INNER))
    return (token_grad.reshape(1, rows, width), proj_grad)


def solution(mesh):
    in_specs = (P("dp", "seq", None), P(), P("dp", "seq", None))
    out_specs = (P("dp", "seq", None), P(("dp", "seq"), None))
    return jax.shard_map(shards, mesh=mesh, in_specs=in_specs, out_specs=out_specs, check_vma=False)
```

```python
import functools
import math

import jax
import jax.numpy as jnp
from jax import lax
from jax.experimental import pallas as pl
from jax.experimental.pallas import tpu as pltpu
from jax.sharding import PartitionSpec as P

MESH = pl.DeviceIdType.MESH
F32 = jnp.float32
BF16 = jnp.bfloat16

HEADS = 8
HD = 128
ROWS = 128
WIDTH = 1024
INNER = HEADS * HD
NX, NY, NZ = 4, 4, 8
CHIPS = NX * NY
CHUNKS = 2
SLICE = 32
FLOWS = 6
GROUPS = 128
STEPS = 4
OWNERS = 8
PIECES = 4

ORDERS = (
    ("xu", "xv", "yu", "yv", "za", "zb", "zc"),
    ("xv", "xu", "yv", "yu", "za", "zb", "zc"),
    ("yu", "yv", "xu", "xv", "za", "zb", "zc"),
    ("yv", "yu", "xv", "xu", "za", "zb", "zc"),
    ("zb", "za", "xv", "xu", "yv", "yu", "zc"),
    ("za", "zb", "xu", "xv", "yu", "yv", "zc"),
)


def bits_of(x, y, z):
    return {
        "xu": (x % 2 + x // 2) % 2,
        "xv": x // 2,
        "yu": (y % 2 + y // 2) % 2,
        "yv": y // 2,
        "za": (z % 2 + (z // 2) % 2) % 2,
        "zb": (z // 2) % 2,
        "zc": z // 4,
    }


def place_of(flow, bits):
    total = bits[ORDERS[flow][0]]
    for step, name in enumerate(ORDERS[flow][1:]):
        total = total + bits[name] * (GROUPS >> (step + 1))
    return total


SHIFTS = sorted(
    ((dx, dy) for dx in range(NX) for dy in range(NY) if (dx, dy) != (0, 0)),
    key=lambda d: -(min(d[0], NX - d[0]) + min(d[1], NY - d[1])),
)


def dot(a, b, dims):
    return lax.dot_general(a, b, (dims, ((), ())), preferred_element_type=F32)


def kernel(
    scale,
    factor,
    tok_hbm,
    w_hbm,
    g_hbm,
    tg_ref,
    pg_ref,
    tok,
    g,
    w,
    proj,
    tokf,
    tkr,
    tkx,
    tokt,
    loc,
    s1b,
    tb,
    r1,
    eb,
    r2,
    s3b,
    lpart,
    st,
    qg,
    qf,
    qr,
    acc,
    rb,
    fin,
    finp,
    fr,
    load_sem,
    pair_send,
    pair_recv,
    tk_send,
    tk_recv,
    p1_send,
    p1_recv,
    p2_send,
    p2_recv,
    q_send,
    q_recv,
    rs_send,
    rs_recv,
    f_send,
    f_recv,
):
    seq = lax.axis_index("seq")
    z = lax.axis_index("dp")
    core = seq % 2
    chip = seq // 2
    y = chip % NY
    x = chip // NY
    other = 1 - core

    def seq_at(cx, cy):
        return (cx * NY + cy) * 2 + core

    partner = (z, seq + 1 - 2 * core)
    near = {
        "xu": (z, seq_at(x + 1 - 2 * (x % 2), y)),
        "xv": (z, seq_at(3 - x, y)),
        "yu": (z, seq_at(x, y + 1 - 2 * (y % 2))),
        "yv": (z, seq_at(x, 3 - y)),
        "za": (z + 1 - 2 * (z % 2), seq),
        "zb": ((z + 2 * (z % 2) - 1 + NZ) % NZ, seq),
        "zc": ((z + 4) % NZ, seq),
    }
    def crossed(device):
        return (device[0], device[1] + 1 - 2 * core)

    def flipped_place(place, name):
        px, py, pz = place
        if name == "xu":
            return (px + 1 - 2 * (px % 2), py, pz)
        if name == "xv":
            return (3 - px, py, pz)
        if name == "yu":
            return (px, py + 1 - 2 * (py % 2), pz)
        if name == "yv":
            return (px, 3 - py, pz)
        if name == "za":
            return (px, py, pz + 1 - 2 * (pz % 2))
        if name == "zb":
            return (px, py, (pz // 4) * 4 + 3 - pz % 4)
        return (px, py, (pz + 4) % NZ)

    def owners(flow):
        first, left, right = ORDERS[flow][0], ORDERS[flow][5], ORDERS[flow][6]
        found = []
        for mask in range(OWNERS):
            place = (x, y, z)
            for name, on in ((first, mask & 1), (left, mask & 2), (right, mask & 4)):
                if on:
                    place = flipped_place(place, name)
            found.append(place)
        return found

    bits = bits_of(x, y, z)
    targets = []
    for dx, dy in SHIFTS:
        tx, ty = (x + dx) % NX, (y + dy) % NY
        targets.append((tx * NY + ty, (z, seq_at(tx, ty))))

    def remote(src, dst, send, recv, device):
        return pltpu.make_async_remote_copy(
            src_ref=src,
            dst_ref=dst,
            send_sem=send,
            recv_sem=recv,
            device_id=device,
            device_id_type=MESH,
        )

    load_tok = pltpu.make_async_copy(tok_hbm, tok, load_sem.at[0])
    load_g = pltpu.make_async_copy(g_hbm, g, load_sem.at[1])
    load_tok.start()
    load_w = []
    for part in range(3):
        cols = pl.ds(part * INNER, INNER)
        load_w.append(
            pltpu.make_async_copy(w_hbm.at[:, cols], w.at[:, cols], load_sem.at[2 + part])
        )
        load_w[part].start()
    load_g.start()

    barrier = pltpu.get_barrier_semaphore()
    greeted = [partner] + [t[1] for t in targets]
    greeted += [crossed(near[order[0]]) for order in ORDERS]
    seen = set()
    for flow in range(FLOWS):
        first, left, right = ORDERS[flow][0], ORDERS[flow][5], ORDERS[flow][6]
        for mask, place in enumerate(owners(flow)):
            flips = [n for n, on in ((first, mask & 1), (left, mask & 2), (right, mask & 4)) if on]
            key = frozenset(flips)
            if any(name[0] == "z" for name in flips) and key not in seen:
                seen.add(key)
                greeted.append((place[2], seq_at(place[0], place[1])))
    greeted.append(near["zb"])
    for device in greeted:
        pl.semaphore_signal(barrier, inc=1, device_id=device, device_id_type=MESH)

    load_tok.wait()

    def own_transpose(i, carry):
        rows = pl.ds(pl.multiple_of(i * 128, 128), 128)
        flipped = tok[:, rows].astype(F32).T
        tokf[rows, :] = flipped
        tokt[rows, 0:128] = flipped.astype(BF16)
        return carry

    lax.fori_loop(0, WIDTH // 128, own_transpose, 0)

    for part in range(3):
        load_w[part].wait()

        def project(i, carry, part=part):
            cols = pl.ds(pl.multiple_of(part * INNER + i * 256, 256), 256)
            proj[:, cols] = dot(tok[...], w[:, cols], ((1,), (0,))).astype(BF16)
            return carry

        lax.fori_loop(0, INNER // 256, project, 0)
    load_g.wait()

    def head_cols(part, h):
        return pl.ds(pl.multiple_of(part * INNER + h * HD, HD), HD)

    pl.semaphore_wait(barrier, len(greeted))
    piece = WIDTH // PIECES
    tokens_out = {}
    relays = {}

    def send_tokens(flows, part):
        rows = pl.ds(part * piece, piece)
        for flow in flows:
            copy = remote(
                tokf.at[rows],
                tkr.at[flow, rows],
                tk_send.at[flow, part],
                tk_recv.at[flow, part],
                near[ORDERS[flow][0]],
            )
            copy.start()
            tokens_out[flow, part] = copy

    def relay_tokens(flows, part):
        rows = pl.ds(part * piece, piece)
        for flow in flows:
            tokens_out[flow, part].wait_recv()
            copy = remote(
                tkr.at[flow, rows],
                tkx.at[flow, rows],
                tk_send.at[FLOWS + flow, part],
                tk_recv.at[FLOWS + flow, part],
                partner,
            )
            copy.start()
            relays[flow, part] = copy

    z_flows, xy_flows = (4, 5), (0, 1, 2, 3)
    send_tokens(xy_flows, 0)
    for part in range(PIECES):
        send_tokens(z_flows, part)

    pair_state = []
    for chunk in range(CHUNKS):

        def local_state(i, carry, chunk=chunk):
            h = 4 * chunk + i
            q = proj[:, head_cols(0, h)]
            k = proj[:, head_cols(1, h)]
            v = proj[:, head_cols(2, h)]
            d = g[:, head_cols(0, h)]
            loc[0, chunk, pl.ds(4 * i, 4)] = dot(k, v, ((0,), (0,))).reshape(4, SLICE, HD)
            loc[1, chunk, pl.ds(4 * i, 4)] = (scale * dot(q, d, ((0,), (0,)))).reshape(4, SLICE, HD)
            return carry

        lax.fori_loop(0, HEADS // CHUNKS, local_state, 0)
        copy = remote(
            loc.at[core, chunk],
            s1b.at[chunk],
            pair_send.at[chunk],
            pair_recv.at[chunk],
            partner,
        )
        copy.start()
        pair_state.append(copy)

    first = []
    for chunk in range(CHUNKS):
        pair_state[chunk].wait_recv()
        tb[chunk] = loc[other, chunk] + s1b[chunk]
        copies = []
        for i, (target, device) in enumerate(targets):
            copy = remote(
                tb.at[chunk, target],
                r1.at[chunk, chip],
                p1_send.at[chunk, i],
                p1_recv.at[chunk, i],
                device,
            )
            copy.start()
            copies.append(copy)
        first.append(copies)
        r1[chunk, chip] = tb[chunk, chip]
    send_tokens(xy_flows, 1)
    send_tok = remote(tokf, tkr.at[FLOWS], pair_send.at[4], pair_recv.at[4], partner)
    send_tok.start()

    row = lax.broadcasted_iota(jnp.int32, (ROWS, ROWS), 0)
    col = lax.broadcasted_iota(jnp.int32, (ROWS, ROWS), 1)
    causal = row >= col

    def inside(h, carry):
        q = proj[:, head_cols(0, h)]
        k = proj[:, head_cols(1, h)]
        v = proj[:, head_cols(2, h)]
        d = g[:, head_cols(0, h)]
        sa = jnp.where(causal, dot(d, v, ((1,), (1,))), 0.0).astype(BF16)
        sb = jnp.where(causal, dot(q, k, ((1,), (1,))), 0.0).astype(BF16)
        lpart[:, head_cols(0, h)] = dot(sa, k, ((1,), (0,)))
        lpart[:, head_cols(1, h)] = dot(sa, q, ((0,), (0,)))
        lpart[:, head_cols(2, h)] = dot(sb, d, ((0,), (0,)))
        return carry

    lax.fori_loop(0, HEADS, inside, 0)

    second = []
    for chunk in range(CHUNKS):
        for copy in first[chunk]:
            copy.wait_recv()
        running = jnp.zeros((SLICE, HD), F32)
        for i in range(CHIPS):
            place = core * i + other * (CHIPS - 1 - i)
            eb[chunk, place] = running
            if i < CHIPS - 1:
                running = running + r1[chunk, place]
        copies = []
        for i, (target, device) in enumerate(targets):
            copy = remote(
                eb.at[chunk, target],
                r2.at[chunk, chip],
                p2_send.at[chunk, i],
                p2_recv.at[chunk, i],
                device,
            )
            copy.start()
            copies.append(copy)
        second.append(copies)
        r2[chunk, chip] = eb[chunk, chip]

    send_tokens(xy_flows, 2)
    send_tokens(xy_flows, 3)
    relay_tokens(xy_flows, 0)
    for part in range(PIECES):
        relay_tokens(z_flows, part)
    send_tok.wait_recv()
    tokt[:, 128:256] = tkr[FLOWS].astype(BF16)

    pair_scan = []
    for chunk in range(CHUNKS):
        for copy in second[chunk]:
            copy.wait_recv()
        copy = remote(
            r2.at[chunk],
            s3b.at[chunk],
            pair_send.at[2 + chunk],
            pair_recv.at[2 + chunk],
            partner,
        )
        copy.start()
        pair_scan.append(copy)
        st[other, chunk] = (r2[chunk] + s1b[chunk]).astype(BF16)

    def finish(h):
        q_cols, k_cols, v_cols = (head_cols(part, h) for part in range(3))
        k = proj[:, k_cols]
        v = proj[:, v_cols]
        d = g[:, q_cols]
        at = 4 * (h % 4)
        prefix = st[0, h // 4, at : at + 4].reshape(HD, HD)
        suffix = st[1, h // 4, at : at + 4].reshape(HD, HD)
        dq = scale * (lpart[:, q_cols] + dot(d, prefix, ((1,), (1,))))
        dk = scale * lpart[:, k_cols] + dot(v, suffix, ((1,), (1,)))
        dv = scale * lpart[:, v_cols] + dot(k, suffix, ((1,), (0,)))
        out = [t.astype(BF16) for t in (dq, dk, dv)]
        for part, (cols, t) in enumerate(zip((q_cols, k_cols, v_cols), out)):
            qg[:, cols] = t
            qf[part, h] = t.astype(F32)

    first_bit = [bits[ORDERS[flow][0]] for flow in range(FLOWS)]

    def head_of(flow, at_core, bit):
        return 4 * (flow % 2) + 2 * at_core + bit

    gather = [None] * FLOWS
    for pair in range(2):
        pair_scan[pair].wait_recv()
        st[core, pair] = s3b[pair].astype(BF16)
        for h in range(4):
            finish(4 * pair + h)
        for part in (2, 1, 0):
            flow = 2 * part + pair
            bit = first_bit[flow]
            link = ORDERS[flow][0]
            copies = []
            for i, (at_core, at_bit, device) in enumerate(
                (
                    (core, 1 - bit, near[link]),
                    (other, 1 - bit, crossed(near[link])),
                    (other, bit, partner),
                )
            ):
                copy = remote(
                    qf.at[part, head_of(flow, at_core, at_bit)],
                    qr.at[flow, i],
                    q_send.at[flow, i],
                    q_recv.at[flow, i],
                    device,
                )
                copy.start()
                copies.append(copy)
            gather[flow] = copies

    for part in (1, 2, 3):
        relay_tokens(xy_flows, part)

    def chip_part(pair):
        blocks = []
        for part in range(3):
            flow = 2 * part + pair
            gather[flow][2].wait_recv()
            own = qg[:, head_cols(part, head_of(flow, core, first_bit[flow]))]
            blocks.append(jnp.concatenate([own, qr[flow, 2].astype(BF16)], axis=0))
        rhs = jnp.concatenate(blocks, axis=1)

        for i in range(NZ):
            out = dot(tokt[i * 128 : i * 128 + 128, :], rhs, ((1,), (0,)))
            for part in range(3):
                flow = 2 * part + pair
                for cx in range(NX):
                    for cy in range(NY):
                        at = 8 * (cx * NY + cy)
                        block = out[at : at + 8, part * 128 : part * 128 + 128]
                        acc[flow, place_of(flow, bits_of(cx, cy, i))] = block

    def halving(flow, step, base):
        size = GROUPS >> (step + 1)
        name = ORDERS[flow][step + 1]
        return remote(
            acc.at[flow, pl.ds(base + (1 - bits[name]) * size, size)],
            rb.at[flow, pl.ds(size, size)],
            rs_send.at[flow, step],
            rs_recv.at[flow, step],
            near[name],
        )

    base = [0] * FLOWS
    steps = []
    current = [None] * FLOWS
    flow_order = (4, 2, 0, 5, 3, 1)
    for flow in flow_order:
        if flow in (4, 5):
            chip_part(flow % 2)
        for part in range(PIECES):
            relays[flow, part].wait_recv()
        gather[flow][0].wait_recv()
        gather[flow][1].wait_recv()
        rhs = jnp.concatenate([qr[flow, 0].astype(BF16), qr[flow, 1].astype(BF16)], axis=0)

        for i in range(NZ):
            rows = pl.ds(i * 128, 128)
            lhs = jnp.concatenate(
                [tkr[flow, rows, :].astype(BF16), tkx[flow, rows, :].astype(BF16)], axis=1
            )
            out = dot(lhs, rhs, ((1,), (0,)))
            for cx in range(NX):
                for cy in range(NY):
                    at = 8 * (cx * NY + cy)
                    place = place_of(flow, bits_of(cx, cy, i))
                    acc[flow, place] = acc[flow, place] + out[at : at + 8]

        current[flow] = halving(flow, 0, 0)
        current[flow].start()
        steps.append(current[flow])

    def token_rows(i, carry):
        rows = pl.ds(pl.multiple_of(i * 256, 256), 256)
        tg_ref[:, rows] = dot(qg[...], w[rows, :], ((1,), (1,))).astype(BF16)
        return carry

    lax.fori_loop(0, WIDTH // 256, token_rows, 0)

    def hand_out(flow):
        copies = [None]
        for mask, place in enumerate(owners(flow)):
            if mask:
                copy = remote(
                    acc.at[flow, place_of(flow, bits_of(*place))],
                    fr.at[flow, mask],
                    f_send.at[flow, mask],
                    f_recv.at[flow, mask],
                    (place[2], seq_at(place[0], place[1])),
                )
                copy.start()
                copies.append(copy)
        return copies

    handed = [None] * FLOWS
    for step in range(STEPS):
        size = GROUPS >> (step + 1)
        for flow in flow_order:
            current[flow].wait_recv()
            base[flow] = base[flow] + bits[ORDERS[flow][step + 1]] * size
            kept = pl.ds(base[flow], size)
            acc[flow, kept] = acc[flow, kept] + rb[flow, size : 2 * size]
            if step + 1 < STEPS:
                current[flow] = halving(flow, step + 1, base[flow])
                current[flow].start()
                steps.append(current[flow])
            else:
                handed[flow] = hand_out(flow)

    for flow in flow_order:
        own = acc[flow, place_of(flow, bits)]
        for copy in handed[flow][1:]:
            copy.wait_recv()
        fin[flow, 0] = (own + fr[flow, 2] + (fr[flow, 4] + fr[flow, 6])) * factor
        fin[flow, 1] = ((fr[flow, 1] + fr[flow, 3]) + (fr[flow, 5] + fr[flow, 7])) * factor

    last = remote(fin, finp, pair_send.at[5], pair_recv.at[5], partner)
    last.start()
    low = core == 0

    def put(at_core, source):
        for flow in range(FLOWS):
            for flip in range(2):
                bit = first_bit[flow] + flip * (1 - 2 * first_bit[flow])
                cols = head_cols(flow // 2, head_of(flow, at_core, bit))
                pg_ref[:, cols] = jnp.where(low, source[flow, flip, 0:4], source[flow, flip, 4:8])

    put(core, fin)
    last.wait_recv()
    put(other, finp)

    for copy in [send_tok, last] + pair_state + pair_scan + steps:
        copy.wait_send()
    for copies in [tokens_out.values(), relays.values()] + first + second:
        for copy in copies:
            copy.wait_send()
    for flow in range(FLOWS):
        for copy in gather[flow] + handed[flow][1:]:
            copy.wait_send()


def shards(tokens, weights, dout):
    rows = tokens.shape[1]
    width = tokens.shape[2]
    seq_count = lax.axis_size("seq")
    data_count = lax.axis_size("dp")
    scale = 1.0 / math.sqrt(HD * rows * seq_count)
    factor = 1.0 / math.sqrt(data_count * rows * seq_count)
    any_space = pl.BlockSpec(memory_space=pl.ANY)
    vmem = pl.BlockSpec(memory_space=pltpu.VMEM)
    slices = (CHUNKS, CHIPS, SLICE, HD)
    dma = pltpu.SemaphoreType.DMA
    token_grad, proj_grad = pl.pallas_call(
        functools.partial(kernel, scale, factor),
        out_shape=(
            jax.ShapeDtypeStruct((rows, width), BF16),
            jax.ShapeDtypeStruct((4, 3 * INNER), F32),
        ),
        in_specs=[any_space] * 3,
        out_specs=(vmem, vmem),
        scratch_shapes=[
            pltpu.VMEM((ROWS, WIDTH), BF16),
            pltpu.VMEM((ROWS, INNER), BF16),
            pltpu.VMEM((WIDTH, 3 * INNER), BF16),
            pltpu.VMEM((ROWS, 3 * INNER), BF16),
            pltpu.VMEM((WIDTH, ROWS), F32),
            pltpu.VMEM((FLOWS + 1, WIDTH, ROWS), F32),
            pltpu.VMEM((FLOWS, WIDTH, ROWS), F32),
            pltpu.VMEM((WIDTH, 2 * ROWS), BF16),
            pltpu.VMEM((2,) + slices, F32),
            pltpu.VMEM(slices, F32),
            pltpu.VMEM(slices, F32),
            pltpu.VMEM(slices, F32),
            pltpu.VMEM(slices, F32),
            pltpu.VMEM(slices, F32),
            pltpu.VMEM(slices, F32),
            pltpu.VMEM((ROWS, 3 * INNER), F32),
            pltpu.VMEM((2,) + slices, BF16),
            pltpu.VMEM((ROWS, 3 * INNER), BF16),
            pltpu.VMEM((3, HEADS, ROWS, HD), F32),
            pltpu.VMEM((FLOWS, 3, ROWS, HD), F32),
            pltpu.VMEM((FLOWS, GROUPS, 8, HD), F32),
            pltpu.VMEM((FLOWS, GROUPS, 8, HD), F32),
            pltpu.VMEM((FLOWS, 2, 8, HD), F32),
            pltpu.VMEM((FLOWS, 2, 8, HD), F32),
            pltpu.VMEM((FLOWS, OWNERS, 8, HD), F32),
            dma((5,)),
            dma((6,)),
            dma((6,)),
            dma((2 * FLOWS, PIECES)),
            dma((2 * FLOWS, PIECES)),
            dma((CHUNKS, CHIPS - 1)),
            dma((CHUNKS, CHIPS - 1)),
            dma((CHUNKS, CHIPS - 1)),
            dma((CHUNKS, CHIPS - 1)),
            dma((FLOWS, 3)),
            dma((FLOWS, 3)),
            dma((FLOWS, STEPS)),
            dma((FLOWS, STEPS)),
            dma((FLOWS, OWNERS)),
            dma((FLOWS, OWNERS)),
        ],
        compiler_params=pltpu.CompilerParams(
            collective_id=0, has_side_effects=True, vmem_limit_bytes=60 * 1024 * 1024
        ),
    )(tokens.reshape(rows, width), weights, dout.reshape(rows, INNER))
    return (token_grad.reshape(1, rows, width), proj_grad)


def solution(mesh):
    in_specs = (P("dp", "seq", None), P(), P("dp", "seq", None))
    out_specs = (P("dp", "seq", None), P(("dp", "seq"), None))
    return jax.shard_map(shards, mesh=mesh, in_specs=in_specs, out_specs=out_specs, check_vma=False)
```

```python
import functools
import math

import jax
import jax.numpy as jnp
from jax import lax
from jax.experimental import pallas as pl
from jax.experimental.pallas import tpu as pltpu
from jax.sharding import PartitionSpec as P

MESH = pl.DeviceIdType.MESH
F32 = jnp.float32
BF16 = jnp.bfloat16

HEADS = 8
HD = 128
ROWS = 128
WIDTH = 1024
INNER = HEADS * HD
NX, NY, NZ = 4, 4, 8
CHIPS = NX * NY
CHUNKS = 2
SLICE = 32
FLOWS = 6
GROUPS = 128
STEPS = 4
OWNERS = 8
PIECES = 4

ORDERS = (
    ("xu", "xv", "yu", "yv", "za", "zb", "zc"),
    ("xv", "xu", "yv", "yu", "za", "zb", "zc"),
    ("yu", "yv", "xu", "xv", "za", "zb", "zc"),
    ("yv", "yu", "xv", "xu", "za", "zb", "zc"),
    ("zb", "za", "xv", "xu", "yv", "yu", "zc"),
    ("za", "zb", "xu", "xv", "yu", "yv", "zc"),
)


def bits_of(x, y, z):
    return {
        "xu": (x % 2 + x // 2) % 2,
        "xv": x // 2,
        "yu": (y % 2 + y // 2) % 2,
        "yv": y // 2,
        "za": (z % 2 + (z // 2) % 2) % 2,
        "zb": (z // 2) % 2,
        "zc": z // 4,
    }


def place_of(flow, bits):
    total = bits[ORDERS[flow][0]]
    for step, name in enumerate(ORDERS[flow][1:]):
        total = total + bits[name] * (GROUPS >> (step + 1))
    return total


SHIFTS = sorted(
    ((dx, dy) for dx in range(NX) for dy in range(NY) if (dx, dy) != (0, 0)),
    key=lambda d: -(min(d[0], NX - d[0]) + min(d[1], NY - d[1])),
)


def dot(a, b, dims):
    return lax.dot_general(a, b, (dims, ((), ())), preferred_element_type=F32)


def kernel(
    scale,
    factor,
    tok_hbm,
    w_hbm,
    g_hbm,
    tg_ref,
    pg_ref,
    tok,
    g,
    w,
    proj,
    tokf,
    tkr,
    tkx,
    tokt,
    loc,
    s1b,
    tb,
    r1,
    eb,
    r2,
    s3b,
    lpart,
    st,
    qg,
    qf,
    qr,
    acc,
    rb,
    fin,
    finp,
    fr,
    load_sem,
    pair_send,
    pair_recv,
    tk_send,
    tk_recv,
    p1_send,
    p1_recv,
    p2_send,
    p2_recv,
    q_send,
    q_recv,
    rs_send,
    rs_recv,
    f_send,
    f_recv,
):
    seq = lax.axis_index("seq")
    z = lax.axis_index("dp")
    core = seq % 2
    chip = seq // 2
    y = chip % NY
    x = chip // NY
    other = 1 - core

    def seq_at(cx, cy):
        return (cx * NY + cy) * 2 + core

    partner = (z, seq + 1 - 2 * core)
    near = {
        "xu": (z, seq_at(x + 1 - 2 * (x % 2), y)),
        "xv": (z, seq_at(3 - x, y)),
        "yu": (z, seq_at(x, y + 1 - 2 * (y % 2))),
        "yv": (z, seq_at(x, 3 - y)),
        "za": (z + 1 - 2 * (z % 2), seq),
        "zb": ((z + 2 * (z % 2) - 1 + NZ) % NZ, seq),
        "zc": ((z + 4) % NZ, seq),
    }
    def crossed(device):
        return (device[0], device[1] + 1 - 2 * core)

    def flipped_place(place, name):
        px, py, pz = place
        if name == "xu":
            return (px + 1 - 2 * (px % 2), py, pz)
        if name == "xv":
            return (3 - px, py, pz)
        if name == "yu":
            return (px, py + 1 - 2 * (py % 2), pz)
        if name == "yv":
            return (px, 3 - py, pz)
        if name == "za":
            return (px, py, pz + 1 - 2 * (pz % 2))
        if name == "zb":
            return (px, py, (pz // 4) * 4 + 3 - pz % 4)
        return (px, py, (pz + 4) % NZ)

    def owners(flow):
        first, left, right = ORDERS[flow][0], ORDERS[flow][5], ORDERS[flow][6]
        found = []
        for mask in range(OWNERS):
            place = (x, y, z)
            for name, on in ((first, mask & 1), (left, mask & 2), (right, mask & 4)):
                if on:
                    place = flipped_place(place, name)
            found.append(place)
        return found

    bits = bits_of(x, y, z)
    targets = []
    for dx, dy in SHIFTS:
        tx, ty = (x + dx) % NX, (y + dy) % NY
        targets.append((tx * NY + ty, (z, seq_at(tx, ty))))

    def remote(src, dst, send, recv, device):
        return pltpu.make_async_remote_copy(
            src_ref=src,
            dst_ref=dst,
            send_sem=send,
            recv_sem=recv,
            device_id=device,
            device_id_type=MESH,
        )

    load_tok = pltpu.make_async_copy(tok_hbm, tok, load_sem.at[0])
    load_g = pltpu.make_async_copy(g_hbm, g, load_sem.at[1])
    load_tok.start()
    load_w = []
    for part in range(3):
        cols = pl.ds(part * INNER, INNER)
        load_w.append(
            pltpu.make_async_copy(w_hbm.at[:, cols], w.at[:, cols], load_sem.at[2 + part])
        )
        load_w[part].start()
    load_g.start()

    barrier = pltpu.get_barrier_semaphore()
    greeted = [partner, near["za"], near["zb"]] + [t[1] for t in targets]
    greeted += [crossed(near[order[0]]) for order in ORDERS]
    for device in greeted:
        pl.semaphore_signal(barrier, inc=1, device_id=device, device_id_type=MESH)

    load_tok.wait()

    def own_transpose(i, carry):
        rows = pl.ds(pl.multiple_of(i * 128, 128), 128)
        flipped = tok[:, rows].astype(F32).T
        tokf[rows, :] = flipped
        tokt[rows, 0:128] = flipped.astype(BF16)
        return carry

    lax.fori_loop(0, WIDTH // 128, own_transpose, 0)

    for part in range(3):
        load_w[part].wait()

        def project(i, carry, part=part):
            cols = pl.ds(pl.multiple_of(part * INNER + i * 256, 256), 256)
            proj[:, cols] = dot(tok[...], w[:, cols], ((1,), (0,))).astype(BF16)
            return carry

        lax.fori_loop(0, INNER // 256, project, 0)
    load_g.wait()

    def head_cols(part, h):
        return pl.ds(pl.multiple_of(part * INNER + h * HD, HD), HD)

    pl.semaphore_wait(barrier, len(greeted))
    piece = WIDTH // PIECES
    tokens_out = {}
    relays = {}

    def send_tokens(flows, part):
        rows = pl.ds(part * piece, piece)
        for flow in flows:
            copy = remote(
                tokf.at[rows],
                tkr.at[flow, rows],
                tk_send.at[flow, part],
                tk_recv.at[flow, part],
                near[ORDERS[flow][0]],
            )
            copy.start()
            tokens_out[flow, part] = copy

    def relay_tokens(flows, part):
        rows = pl.ds(part * piece, piece)
        for flow in flows:
            tokens_out[flow, part].wait_recv()
            copy = remote(
                tkr.at[flow, rows],
                tkx.at[flow, rows],
                tk_send.at[FLOWS + flow, part],
                tk_recv.at[FLOWS + flow, part],
                partner,
            )
            copy.start()
            relays[flow, part] = copy

    z_flows, xy_flows = (4, 5), (0, 1, 2, 3)
    send_tokens(xy_flows, 0)
    for part in range(PIECES):
        send_tokens(z_flows, part)

    pair_state = []
    for chunk in range(CHUNKS):

        for i in range(HEADS // CHUNKS):
            h = 4 * chunk + i
            q = proj[:, head_cols(0, h)]
            k = proj[:, head_cols(1, h)]
            v = proj[:, head_cols(2, h)]
            d = g[:, head_cols(0, h)]
            loc[0, chunk, 4 * i : 4 * i + 4] = dot(k, v, ((0,), (0,))).reshape(4, SLICE, HD)
            loc[1, chunk, 4 * i : 4 * i + 4] = (scale * dot(q, d, ((0,), (0,)))).reshape(4, SLICE, HD)

        copy = remote(
            loc.at[core, chunk],
            s1b.at[chunk],
            pair_send.at[chunk],
            pair_recv.at[chunk],
            partner,
        )
        copy.start()
        pair_state.append(copy)

    first = []
    for chunk in range(CHUNKS):
        pair_state[chunk].wait_recv()
        tb[chunk] = loc[other, chunk] + s1b[chunk]
        copies = []
        for i, (target, device) in enumerate(targets):
            copy = remote(
                tb.at[chunk, target],
                r1.at[chunk, chip],
                p1_send.at[chunk, i],
                p1_recv.at[chunk, i],
                device,
            )
            copy.start()
            copies.append(copy)
        first.append(copies)
        r1[chunk, chip] = tb[chunk, chip]
    send_tokens(xy_flows, 1)
    send_tok = remote(tokf, tkr.at[FLOWS], pair_send.at[4], pair_recv.at[4], partner)
    send_tok.start()

    row = lax.broadcasted_iota(jnp.int32, (ROWS, ROWS), 0)
    col = lax.broadcasted_iota(jnp.int32, (ROWS, ROWS), 1)
    causal = row >= col

    def inside(h, carry):
        q = proj[:, head_cols(0, h)]
        k = proj[:, head_cols(1, h)]
        v = proj[:, head_cols(2, h)]
        d = g[:, head_cols(0, h)]
        sa = jnp.where(causal, dot(d, v, ((1,), (1,))), 0.0).astype(BF16)
        sb = jnp.where(causal, dot(q, k, ((1,), (1,))), 0.0).astype(BF16)
        lpart[:, head_cols(0, h)] = dot(sa, k, ((1,), (0,)))
        lpart[:, head_cols(1, h)] = dot(sa, q, ((0,), (0,)))
        lpart[:, head_cols(2, h)] = dot(sb, d, ((0,), (0,)))
        return carry

    lax.fori_loop(0, HEADS, inside, 0)

    second = []
    for chunk in range(CHUNKS):
        for copy in first[chunk]:
            copy.wait_recv()
        running = jnp.zeros((SLICE, HD), F32)
        for i in range(CHIPS):
            place = core * i + other * (CHIPS - 1 - i)
            eb[chunk, place] = running
            if i < CHIPS - 1:
                running = running + r1[chunk, place]
        copies = []
        for i, (target, device) in enumerate(targets):
            copy = remote(
                eb.at[chunk, target],
                r2.at[chunk, chip],
                p2_send.at[chunk, i],
                p2_recv.at[chunk, i],
                device,
            )
            copy.start()
            copies.append(copy)
        second.append(copies)
        r2[chunk, chip] = eb[chunk, chip]

    send_tokens(xy_flows, 2)
    send_tokens(xy_flows, 3)
    relay_tokens(xy_flows, 0)
    for part in range(PIECES):
        relay_tokens(z_flows, part)
    send_tok.wait_recv()
    tokt[:, 128:256] = tkr[FLOWS].astype(BF16)

    pair_scan = []
    for chunk in range(CHUNKS):
        for copy in second[chunk]:
            copy.wait_recv()
        copy = remote(
            r2.at[chunk],
            s3b.at[chunk],
            pair_send.at[2 + chunk],
            pair_recv.at[2 + chunk],
            partner,
        )
        copy.start()
        pair_scan.append(copy)
        st[other, chunk] = (r2[chunk] + s1b[chunk]).astype(BF16)

    def finish(h):
        q_cols, k_cols, v_cols = (head_cols(part, h) for part in range(3))
        k = proj[:, k_cols]
        v = proj[:, v_cols]
        d = g[:, q_cols]
        at = 4 * (h % 4)
        prefix = st[0, h // 4, at : at + 4].reshape(HD, HD)
        suffix = st[1, h // 4, at : at + 4].reshape(HD, HD)
        dq = scale * (lpart[:, q_cols] + dot(d, prefix, ((1,), (1,))))
        dk = scale * lpart[:, k_cols] + dot(v, suffix, ((1,), (1,)))
        dv = scale * lpart[:, v_cols] + dot(k, suffix, ((1,), (0,)))
        out = [t.astype(BF16) for t in (dq, dk, dv)]
        for part, (cols, t) in enumerate(zip((q_cols, k_cols, v_cols), out)):
            qg[:, cols] = t
            qf[part, h] = t.astype(F32)

    first_bit = [bits[ORDERS[flow][0]] for flow in range(FLOWS)]

    def head_of(flow, at_core, bit):
        return 4 * (flow % 2) + 2 * at_core + bit

    gather = [None] * FLOWS
    for pair in range(2):
        pair_scan[pair].wait_recv()
        st[core, pair] = s3b[pair].astype(BF16)
        for h in range(4):
            finish(4 * pair + h)
        for part in (2, 1, 0):
            flow = 2 * part + pair
            bit = first_bit[flow]
            link = ORDERS[flow][0]
            copies = []
            for i, (at_core, at_bit, device) in enumerate(
                (
                    (core, 1 - bit, near[link]),
                    (other, 1 - bit, crossed(near[link])),
                    (other, bit, partner),
                )
            ):
                copy = remote(
                    qf.at[part, head_of(flow, at_core, at_bit)],
                    qr.at[flow, i],
                    q_send.at[flow, i],
                    q_recv.at[flow, i],
                    device,
                )
                copy.start()
                copies.append(copy)
            gather[flow] = copies

    for part in (1, 2, 3):
        relay_tokens(xy_flows, part)

    def chip_part(pair):
        blocks = []
        for part in range(3):
            flow = 2 * part + pair
            gather[flow][2].wait_recv()
            own = qg[:, head_cols(part, head_of(flow, core, first_bit[flow]))]
            blocks.append(jnp.concatenate([own, qr[flow, 2].astype(BF16)], axis=0))
        rhs = jnp.concatenate(blocks, axis=1)

        for i in range(NZ):
            out = dot(tokt[i * 128 : i * 128 + 128, :], rhs, ((1,), (0,)))
            for part in range(3):
                flow = 2 * part + pair
                for cx in range(NX):
                    for cy in range(NY):
                        at = 8 * (cx * NY + cy)
                        block = out[at : at + 8, part * 128 : part * 128 + 128]
                        acc[flow, place_of(flow, bits_of(cx, cy, i))] = block

    def halving(flow, step, base):
        size = GROUPS >> (step + 1)
        name = ORDERS[flow][step + 1]
        return remote(
            acc.at[flow, pl.ds(base + (1 - bits[name]) * size, size)],
            rb.at[flow, pl.ds(size, size)],
            rs_send.at[flow, step],
            rs_recv.at[flow, step],
            near[name],
        )

    base = [0] * FLOWS
    steps = []
    current = [None] * FLOWS
    flow_order = (2, 0, 4, 5, 3, 1)
    for flow in flow_order:
        if flow in (2, 5):
            chip_part(flow % 2)
        for part in range(PIECES):
            relays[flow, part].wait_recv()
        gather[flow][0].wait_recv()
        gather[flow][1].wait_recv()
        rhs = jnp.concatenate([qr[flow, 0].astype(BF16), qr[flow, 1].astype(BF16)], axis=0)

        for i in range(NZ):
            rows = pl.ds(i * 128, 128)
            lhs = jnp.concatenate(
                [tkr[flow, rows, :].astype(BF16), tkx[flow, rows, :].astype(BF16)], axis=1
            )
            out = dot(lhs, rhs, ((1,), (0,)))
            for cx in range(NX):
                for cy in range(NY):
                    at = 8 * (cx * NY + cy)
                    place = place_of(flow, bits_of(cx, cy, i))
                    acc[flow, place] = acc[flow, place] + out[at : at + 8]

        current[flow] = halving(flow, 0, 0)
        current[flow].start()
        steps.append(current[flow])

    def token_rows(i, carry):
        rows = pl.ds(pl.multiple_of(i * 256, 256), 256)
        tg_ref[:, rows] = dot(qg[...], w[rows, :], ((1,), (1,))).astype(BF16)
        return carry

    lax.fori_loop(0, WIDTH // 256, token_rows, 0)

    def hand_out(flow):
        copies = [None]
        for mask, place in enumerate(owners(flow)):
            if mask:
                copy = remote(
                    acc.at[flow, place_of(flow, bits_of(*place))],
                    fr.at[flow, mask],
                    f_send.at[flow, mask],
                    f_recv.at[flow, mask],
                    (place[2], seq_at(place[0], place[1])),
                )
                copy.start()
                copies.append(copy)
        return copies

    handed = [None] * FLOWS
    for step in range(STEPS):
        size = GROUPS >> (step + 1)
        for flow in flow_order if step + 1 < STEPS else (2, 0, 3, 1, 4, 5):
            current[flow].wait_recv()
            base[flow] = base[flow] + bits[ORDERS[flow][step + 1]] * size
            kept = pl.ds(base[flow], size)
            acc[flow, kept] = acc[flow, kept] + rb[flow, size : 2 * size]
            if step + 1 < STEPS:
                current[flow] = halving(flow, step + 1, base[flow])
                current[flow].start()
                steps.append(current[flow])
            else:
                handed[flow] = hand_out(flow)

    for flow in flow_order:
        own = acc[flow, place_of(flow, bits)]
        for copy in handed[flow][1:]:
            copy.wait_recv()
        fin[flow, 0] = (own + fr[flow, 2] + (fr[flow, 4] + fr[flow, 6])) * factor
        fin[flow, 1] = ((fr[flow, 1] + fr[flow, 3]) + (fr[flow, 5] + fr[flow, 7])) * factor

    last = remote(fin, finp, pair_send.at[5], pair_recv.at[5], partner)
    last.start()
    low = core == 0

    def put(at_core, source):
        for flow in range(FLOWS):
            for flip in range(2):
                bit = first_bit[flow] + flip * (1 - 2 * first_bit[flow])
                cols = head_cols(flow // 2, head_of(flow, at_core, bit))
                pg_ref[:, cols] = jnp.where(low, source[flow, flip, 0:4], source[flow, flip, 4:8])

    put(core, fin)
    last.wait_recv()
    put(other, finp)

    for copy in [send_tok, last] + pair_state + pair_scan + steps:
        copy.wait_send()
    for copies in [tokens_out.values(), relays.values()] + first + second:
        for copy in copies:
            copy.wait_send()
    for flow in range(FLOWS):
        for copy in gather[flow] + handed[flow][1:]:
            copy.wait_send()


def shards(tokens, weights, dout):
    rows = tokens.shape[1]
    width = tokens.shape[2]
    seq_count = lax.axis_size("seq")
    data_count = lax.axis_size("dp")
    scale = 1.0 / math.sqrt(HD * rows * seq_count)
    factor = 1.0 / math.sqrt(data_count * rows * seq_count)
    any_space = pl.BlockSpec(memory_space=pl.ANY)
    vmem = pl.BlockSpec(memory_space=pltpu.VMEM)
    slices = (CHUNKS, CHIPS, SLICE, HD)
    dma = pltpu.SemaphoreType.DMA
    token_grad, proj_grad = pl.pallas_call(
        functools.partial(kernel, scale, factor),
        out_shape=(
            jax.ShapeDtypeStruct((rows, width), BF16),
            jax.ShapeDtypeStruct((4, 3 * INNER), F32),
        ),
        in_specs=[any_space] * 3,
        out_specs=(vmem, vmem),
        scratch_shapes=[
            pltpu.VMEM((ROWS, WIDTH), BF16),
            pltpu.VMEM((ROWS, INNER), BF16),
            pltpu.VMEM((WIDTH, 3 * INNER), BF16),
            pltpu.VMEM((ROWS, 3 * INNER), BF16),
            pltpu.VMEM((WIDTH, ROWS), F32),
            pltpu.VMEM((FLOWS + 1, WIDTH, ROWS), F32),
            pltpu.VMEM((FLOWS, WIDTH, ROWS), F32),
            pltpu.VMEM((WIDTH, 2 * ROWS), BF16),
            pltpu.VMEM((2,) + slices, F32),
            pltpu.VMEM(slices, F32),
            pltpu.VMEM(slices, F32),
            pltpu.VMEM(slices, F32),
            pltpu.VMEM(slices, F32),
            pltpu.VMEM(slices, F32),
            pltpu.VMEM(slices, F32),
            pltpu.VMEM((ROWS, 3 * INNER), F32),
            pltpu.VMEM((2,) + slices, BF16),
            pltpu.VMEM((ROWS, 3 * INNER), BF16),
            pltpu.VMEM((3, HEADS, ROWS, HD), F32),
            pltpu.VMEM((FLOWS, 3, ROWS, HD), F32),
            pltpu.VMEM((FLOWS, GROUPS, 8, HD), F32),
            pltpu.VMEM((FLOWS, GROUPS, 8, HD), F32),
            pltpu.VMEM((FLOWS, 2, 8, HD), F32),
            pltpu.VMEM((FLOWS, 2, 8, HD), F32),
            pltpu.VMEM((FLOWS, OWNERS, 8, HD), F32),
            dma((5,)),
            dma((6,)),
            dma((6,)),
            dma((2 * FLOWS, PIECES)),
            dma((2 * FLOWS, PIECES)),
            dma((CHUNKS, CHIPS - 1)),
            dma((CHUNKS, CHIPS - 1)),
            dma((CHUNKS, CHIPS - 1)),
            dma((CHUNKS, CHIPS - 1)),
            dma((FLOWS, 3)),
            dma((FLOWS, 3)),
            dma((FLOWS, STEPS)),
            dma((FLOWS, STEPS)),
            dma((FLOWS, OWNERS)),
            dma((FLOWS, OWNERS)),
        ],
        compiler_params=pltpu.CompilerParams(
            collective_id=0, has_side_effects=True, vmem_limit_bytes=60 * 1024 * 1024
        ),
    )(tokens.reshape(rows, width), weights, dout.reshape(rows, INNER))
    return (token_grad.reshape(1, rows, width), proj_grad)


def solution(mesh):
    in_specs = (P("dp", "seq", None), P(), P("dp", "seq", None))
    out_specs = (P("dp", "seq", None), P(("dp", "seq"), None))
    return jax.shard_map(shards, mesh=mesh, in_specs=in_specs, out_specs=out_specs, check_vma=False)
```

```python
import functools
import math

import jax
import jax.numpy as jnp
from jax import lax
from jax.experimental import pallas as pl
from jax.experimental.pallas import tpu as pltpu
from jax.sharding import PartitionSpec as P

MESH = pl.DeviceIdType.MESH
F32 = jnp.float32
BF16 = jnp.bfloat16

HEADS = 8
HD = 128
ROWS = 128
WIDTH = 1024
INNER = HEADS * HD
NX, NY, NZ = 4, 4, 8
CHIPS = NX * NY
CHUNKS = 2
SLICE = 32
FLOWS = 6
GROUPS = 128
STEPS = 4
OWNERS = 8
PIECES = 4

ORDERS = (
    ("xu", "xv", "yu", "yv", "za", "zb", "zc"),
    ("xv", "xu", "yv", "yu", "za", "zb", "zc"),
    ("yu", "yv", "xu", "xv", "za", "zb", "zc"),
    ("yv", "yu", "xv", "xu", "za", "zb", "zc"),
    ("zb", "za", "xv", "xu", "yv", "yu", "zc"),
    ("za", "zb", "xu", "xv", "yu", "yv", "zc"),
)


def bits_of(x, y, z):
    return {
        "xu": (x % 2 + x // 2) % 2,
        "xv": x // 2,
        "yu": (y % 2 + y // 2) % 2,
        "yv": y // 2,
        "za": (z % 2 + (z // 2) % 2) % 2,
        "zb": (z // 2) % 2,
        "zc": z // 4,
    }


def place_of(flow, bits):
    total = bits[ORDERS[flow][0]]
    for step, name in enumerate(ORDERS[flow][1:]):
        total = total + bits[name] * (GROUPS >> (step + 1))
    return total


SHIFTS = sorted(
    ((dx, dy) for dx in range(NX) for dy in range(NY) if (dx, dy) != (0, 0)),
    key=lambda d: -(min(d[0], NX - d[0]) + min(d[1], NY - d[1])),
)


def dot(a, b, dims):
    return lax.dot_general(a, b, (dims, ((), ())), preferred_element_type=F32)


def kernel(
    scale,
    factor,
    tok_hbm,
    w_hbm,
    g_hbm,
    tg_ref,
    pg_ref,
    tok,
    g,
    w,
    proj,
    tokf,
    tkr,
    tkx,
    tokt,
    loc,
    s1b,
    tb,
    r1,
    eb,
    r2,
    s3b,
    lpart,
    st,
    qg,
    qf,
    qr,
    acc,
    rb,
    fin,
    finp,
    fr,
    load_sem,
    pair_send,
    pair_recv,
    tk_send,
    tk_recv,
    p1_send,
    p1_recv,
    p2_send,
    p2_recv,
    q_send,
    q_recv,
    rs_send,
    rs_recv,
    f_send,
    f_recv,
):
    seq = lax.axis_index("seq")
    z = lax.axis_index("dp")
    core = seq % 2
    chip = seq // 2
    y = chip % NY
    x = chip // NY
    other = 1 - core

    def seq_at(cx, cy):
        return (cx * NY + cy) * 2 + core

    partner = (z, seq + 1 - 2 * core)
    near = {
        "xu": (z, seq_at(x + 1 - 2 * (x % 2), y)),
        "xv": (z, seq_at(3 - x, y)),
        "yu": (z, seq_at(x, y + 1 - 2 * (y % 2))),
        "yv": (z, seq_at(x, 3 - y)),
        "za": (z + 1 - 2 * (z % 2), seq),
        "zb": ((z + 2 * (z % 2) - 1 + NZ) % NZ, seq),
        "zc": ((z + 4) % NZ, seq),
    }
    def crossed(device):
        return (device[0], device[1] + 1 - 2 * core)

    def flipped_place(place, name):
        px, py, pz = place
        if name == "xu":
            return (px + 1 - 2 * (px % 2), py, pz)
        if name == "xv":
            return (3 - px, py, pz)
        if name == "yu":
            return (px, py + 1 - 2 * (py % 2), pz)
        if name == "yv":
            return (px, 3 - py, pz)
        if name == "za":
            return (px, py, pz + 1 - 2 * (pz % 2))
        if name == "zb":
            return (px, py, (pz // 4) * 4 + 3 - pz % 4)
        return (px, py, (pz + 4) % NZ)

    def owners(flow):
        first, left, right = ORDERS[flow][0], ORDERS[flow][5], ORDERS[flow][6]
        found = []
        for mask in range(OWNERS):
            place = (x, y, z)
            for name, on in ((first, mask & 1), (left, mask & 2), (right, mask & 4)):
                if on:
                    place = flipped_place(place, name)
            found.append(place)
        return found

    bits = bits_of(x, y, z)
    targets = []
    for dx, dy in SHIFTS:
        tx, ty = (x + dx) % NX, (y + dy) % NY
        targets.append((tx * NY + ty, (z, seq_at(tx, ty))))

    def remote(src, dst, send, recv, device):
        return pltpu.make_async_remote_copy(
            src_ref=src,
            dst_ref=dst,
            send_sem=send,
            recv_sem=recv,
            device_id=device,
            device_id_type=MESH,
        )

    load_tok = pltpu.make_async_copy(tok_hbm, tok, load_sem.at[0])
    load_g = pltpu.make_async_copy(g_hbm, g, load_sem.at[1])
    load_tok.start()
    load_w = []
    for part in range(3):
        cols = pl.ds(part * INNER, INNER)
        load_w.append(
            pltpu.make_async_copy(w_hbm.at[:, cols], w.at[:, cols], load_sem.at[2 + part])
        )
        load_w[part].start()
    load_g.start()

    barrier = pltpu.get_barrier_semaphore()
    greeted = [partner, near["za"], near["zb"]] + [t[1] for t in targets]
    greeted += [crossed(near[order[0]]) for order in ORDERS]
    for device in greeted:
        pl.semaphore_signal(barrier, inc=1, device_id=device, device_id_type=MESH)

    load_tok.wait()

    def own_transpose(i, carry):
        rows = pl.ds(pl.multiple_of(i * 128, 128), 128)
        flipped = tok[:, rows].astype(F32).T
        tokf[rows, :] = flipped
        tokt[rows, 0:128] = flipped.astype(BF16)
        return carry

    lax.fori_loop(0, WIDTH // 128, own_transpose, 0)

    for part in range(3):
        load_w[part].wait()

        def project(i, carry, part=part):
            cols = pl.ds(pl.multiple_of(part * INNER + i * 256, 256), 256)
            proj[:, cols] = dot(tok[...], w[:, cols], ((1,), (0,))).astype(BF16)
            return carry

        lax.fori_loop(0, INNER // 256, project, 0, unroll=True)
    load_g.wait()

    def head_cols(part, h):
        return pl.ds(pl.multiple_of(part * INNER + h * HD, HD), HD)

    pl.semaphore_wait(barrier, len(greeted))
    piece = WIDTH // PIECES
    tokens_out = {}
    relays = {}

    def send_tokens(flows, part):
        rows = pl.ds(part * piece, piece)
        for flow in flows:
            copy = remote(
                tokf.at[rows],
                tkr.at[flow, rows],
                tk_send.at[flow, part],
                tk_recv.at[flow, part],
                near[ORDERS[flow][0]],
            )
            copy.start()
            tokens_out[flow, part] = copy

    def relay_tokens(flows, part):
        rows = pl.ds(part * piece, piece)
        for flow in flows:
            tokens_out[flow, part].wait_recv()
            copy = remote(
                tkr.at[flow, rows],
                tkx.at[flow, rows],
                tk_send.at[FLOWS + flow, part],
                tk_recv.at[FLOWS + flow, part],
                partner,
            )
            copy.start()
            relays[flow, part] = copy

    z_flows, xy_flows = (4, 5), (0, 1, 2, 3)
    send_tokens(xy_flows, 0)
    for part in range(PIECES):
        send_tokens(z_flows, part)

    pair_state = []
    for chunk in range(CHUNKS):

        for i in range(HEADS // CHUNKS):
            h = 4 * chunk + i
            q = proj[:, head_cols(0, h)]
            k = proj[:, head_cols(1, h)]
            v = proj[:, head_cols(2, h)]
            d = g[:, head_cols(0, h)]
            loc[0, chunk, 4 * i : 4 * i + 4] = dot(k, v, ((0,), (0,))).reshape(4, SLICE, HD)
            loc[1, chunk, 4 * i : 4 * i + 4] = (scale * dot(q, d, ((0,), (0,)))).reshape(4, SLICE, HD)

        copy = remote(
            loc.at[core, chunk],
            s1b.at[chunk],
            pair_send.at[chunk],
            pair_recv.at[chunk],
            partner,
        )
        copy.start()
        pair_state.append(copy)

    first = []
    for chunk in range(CHUNKS):
        pair_state[chunk].wait_recv()
        tb[chunk] = loc[other, chunk] + s1b[chunk]
        copies = []
        for i, (target, device) in enumerate(targets):
            copy = remote(
                tb.at[chunk, target],
                r1.at[chunk, chip],
                p1_send.at[chunk, i],
                p1_recv.at[chunk, i],
                device,
            )
            copy.start()
            copies.append(copy)
        first.append(copies)
        r1[chunk, chip] = tb[chunk, chip]
    send_tokens(xy_flows, 1)
    send_tok = remote(tokf, tkr.at[FLOWS], pair_send.at[4], pair_recv.at[4], partner)
    send_tok.start()

    row = lax.broadcasted_iota(jnp.int32, (ROWS, ROWS), 0)
    col = lax.broadcasted_iota(jnp.int32, (ROWS, ROWS), 1)
    causal = row >= col

    def inside(h, carry):
        q = proj[:, head_cols(0, h)]
        k = proj[:, head_cols(1, h)]
        v = proj[:, head_cols(2, h)]
        d = g[:, head_cols(0, h)]
        sa = jnp.where(causal, dot(d, v, ((1,), (1,))), 0.0).astype(BF16)
        sb = jnp.where(causal, dot(q, k, ((1,), (1,))), 0.0).astype(BF16)
        lpart[:, head_cols(0, h)] = dot(sa, k, ((1,), (0,)))
        lpart[:, head_cols(1, h)] = dot(sa, q, ((0,), (0,)))
        lpart[:, head_cols(2, h)] = dot(sb, d, ((0,), (0,)))
        return carry

    lax.fori_loop(0, HEADS, inside, 0)

    second = []
    for chunk in range(CHUNKS):
        for copy in first[chunk]:
            copy.wait_recv()
        running = jnp.zeros((SLICE, HD), F32)
        for i in range(CHIPS):
            place = core * i + other * (CHIPS - 1 - i)
            eb[chunk, place] = running
            if i < CHIPS - 1:
                running = running + r1[chunk, place]
        copies = []
        for i, (target, device) in enumerate(targets):
            copy = remote(
                eb.at[chunk, target],
                r2.at[chunk, chip],
                p2_send.at[chunk, i],
                p2_recv.at[chunk, i],
                device,
            )
            copy.start()
            copies.append(copy)
        second.append(copies)
        r2[chunk, chip] = eb[chunk, chip]

    send_tokens(xy_flows, 2)
    send_tokens(xy_flows, 3)
    relay_tokens(xy_flows, 0)
    for part in range(PIECES):
        relay_tokens(z_flows, part)
    send_tok.wait_recv()
    tokt[:, 128:256] = tkr[FLOWS].astype(BF16)

    pair_scan = []
    for chunk in range(CHUNKS):
        for copy in second[chunk]:
            copy.wait_recv()
        copy = remote(
            r2.at[chunk],
            s3b.at[chunk],
            pair_send.at[2 + chunk],
            pair_recv.at[2 + chunk],
            partner,
        )
        copy.start()
        pair_scan.append(copy)
        st[other, chunk] = (r2[chunk] + s1b[chunk]).astype(BF16)

    def finish(h):
        q_cols, k_cols, v_cols = (head_cols(part, h) for part in range(3))
        k = proj[:, k_cols]
        v = proj[:, v_cols]
        d = g[:, q_cols]
        at = 4 * (h % 4)
        prefix = st[0, h // 4, at : at + 4].reshape(HD, HD)
        suffix = st[1, h // 4, at : at + 4].reshape(HD, HD)
        dq = scale * (lpart[:, q_cols] + dot(d, prefix, ((1,), (1,))))
        dk = scale * lpart[:, k_cols] + dot(v, suffix, ((1,), (1,)))
        dv = scale * lpart[:, v_cols] + dot(k, suffix, ((1,), (0,)))
        out = [t.astype(BF16) for t in (dq, dk, dv)]
        for part, (cols, t) in enumerate(zip((q_cols, k_cols, v_cols), out)):
            qg[:, cols] = t
            qf[part, h] = t.astype(F32)

    first_bit = [bits[ORDERS[flow][0]] for flow in range(FLOWS)]

    def head_of(flow, at_core, bit):
        return 4 * (flow % 2) + 2 * at_core + bit

    gather = [None] * FLOWS
    for pair in range(2):
        pair_scan[pair].wait_recv()
        st[core, pair] = s3b[pair].astype(BF16)
        for h in range(4):
            finish(4 * pair + h)
        for part in (2, 1, 0):
            flow = 2 * part + pair
            bit = first_bit[flow]
            link = ORDERS[flow][0]
            copies = []
            for i, (at_core, at_bit, device) in enumerate(
                (
                    (core, 1 - bit, near[link]),
                    (other, 1 - bit, crossed(near[link])),
                    (other, bit, partner),
                )
            ):
                copy = remote(
                    qf.at[part, head_of(flow, at_core, at_bit)],
                    qr.at[flow, i],
                    q_send.at[flow, i],
                    q_recv.at[flow, i],
                    device,
                )
                copy.start()
                copies.append(copy)
            gather[flow] = copies

    for part in (1, 2, 3):
        relay_tokens(xy_flows, part)

    def chip_part(pair):
        blocks = []
        for part in range(3):
            flow = 2 * part + pair
            gather[flow][2].wait_recv()
            own = qg[:, head_cols(part, head_of(flow, core, first_bit[flow]))]
            blocks.append(jnp.concatenate([own, qr[flow, 2].astype(BF16)], axis=0))
        rhs = jnp.concatenate(blocks, axis=1)

        for i in range(NZ):
            out = dot(tokt[i * 128 : i * 128 + 128, :], rhs, ((1,), (0,)))
            for part in range(3):
                flow = 2 * part + pair
                for cx in range(NX):
                    for cy in range(NY):
                        at = 8 * (cx * NY + cy)
                        block = out[at : at + 8, part * 128 : part * 128 + 128]
                        acc[flow, place_of(flow, bits_of(cx, cy, i))] = block

    def halving(flow, step, base):
        size = GROUPS >> (step + 1)
        name = ORDERS[flow][step + 1]
        return remote(
            acc.at[flow, pl.ds(base + (1 - bits[name]) * size, size)],
            rb.at[flow, pl.ds(size, size)],
            rs_send.at[flow, step],
            rs_recv.at[flow, step],
            near[name],
        )

    base = [0] * FLOWS
    steps = []
    current = [None] * FLOWS
    flow_order = (2, 0, 4, 5, 3, 1)
    for flow in flow_order:
        if flow in (2, 5):
            chip_part(flow % 2)
        for part in range(PIECES):
            relays[flow, part].wait_recv()
        gather[flow][0].wait_recv()
        gather[flow][1].wait_recv()
        rhs = jnp.concatenate([qr[flow, 0].astype(BF16), qr[flow, 1].astype(BF16)], axis=0)

        for i in range(NZ):
            rows = pl.ds(i * 128, 128)
            lhs = jnp.concatenate(
                [tkr[flow, rows, :].astype(BF16), tkx[flow, rows, :].astype(BF16)], axis=1
            )
            out = dot(lhs, rhs, ((1,), (0,)))
            for cx in range(NX):
                for cy in range(NY):
                    at = 8 * (cx * NY + cy)
                    place = place_of(flow, bits_of(cx, cy, i))
                    acc[flow, place] = acc[flow, place] + out[at : at + 8]

        current[flow] = halving(flow, 0, 0)
        current[flow].start()
        steps.append(current[flow])

    def token_rows(i, carry):
        rows = pl.ds(pl.multiple_of(i * 256, 256), 256)
        tg_ref[:, rows] = dot(qg[...], w[rows, :], ((1,), (1,))).astype(BF16)
        return carry

    lax.fori_loop(0, WIDTH // 256, token_rows, 0)

    def hand_out(flow):
        copies = [None]
        for mask, place in enumerate(owners(flow)):
            if mask:
                copy = remote(
                    acc.at[flow, place_of(flow, bits_of(*place))],
                    fr.at[flow, mask],
                    f_send.at[flow, mask],
                    f_recv.at[flow, mask],
                    (place[2], seq_at(place[0], place[1])),
                )
                copy.start()
                copies.append(copy)
        return copies

    handed = [None] * FLOWS
    for step in range(STEPS):
        size = GROUPS >> (step + 1)
        for flow in flow_order if step + 1 < STEPS else (2, 0, 3, 1, 4, 5):
            current[flow].wait_recv()
            base[flow] = base[flow] + bits[ORDERS[flow][step + 1]] * size
            kept = pl.ds(base[flow], size)
            acc[flow, kept] = acc[flow, kept] + rb[flow, size : 2 * size]
            if step + 1 < STEPS:
                current[flow] = halving(flow, step + 1, base[flow])
                current[flow].start()
                steps.append(current[flow])
            else:
                handed[flow] = hand_out(flow)

    for flow in flow_order:
        own = acc[flow, place_of(flow, bits)]
        for copy in handed[flow][1:]:
            copy.wait_recv()
        fin[flow, 0] = (own + fr[flow, 2] + (fr[flow, 4] + fr[flow, 6])) * factor
        fin[flow, 1] = ((fr[flow, 1] + fr[flow, 3]) + (fr[flow, 5] + fr[flow, 7])) * factor

    last = remote(fin, finp, pair_send.at[5], pair_recv.at[5], partner)
    last.start()
    low = core == 0

    def put(at_core, source):
        for flow in range(FLOWS):
            for flip in range(2):
                bit = first_bit[flow] + flip * (1 - 2 * first_bit[flow])
                cols = head_cols(flow // 2, head_of(flow, at_core, bit))
                pg_ref[:, cols] = jnp.where(low, source[flow, flip, 0:4], source[flow, flip, 4:8])

    put(core, fin)
    last.wait_recv()
    put(other, finp)

    for copy in [send_tok, last] + pair_state + pair_scan + steps:
        copy.wait_send()
    for copies in [tokens_out.values(), relays.values()] + first + second:
        for copy in copies:
            copy.wait_send()
    for flow in range(FLOWS):
        for copy in gather[flow] + handed[flow][1:]:
            copy.wait_send()


def settle(tg_in, pg_in, tg_out, pg_out, tg, pg, sem_in, sem_out):
    ins = [
        pltpu.make_async_copy(tg_in, tg, sem_in.at[0]),
        pltpu.make_async_copy(pg_in, pg, sem_in.at[1]),
    ]
    outs = [
        pltpu.make_async_copy(tg, tg_out, sem_out.at[0]),
        pltpu.make_async_copy(pg, pg_out, sem_out.at[1]),
    ]
    for copy in ins:
        copy.start()
    for copy, out in zip(ins, outs):
        copy.wait()
        out.start()
    for out in outs:
        out.wait()


def shards(tokens, weights, dout):
    rows = tokens.shape[1]
    width = tokens.shape[2]
    seq_count = lax.axis_size("seq")
    data_count = lax.axis_size("dp")
    scale = 1.0 / math.sqrt(HD * rows * seq_count)
    factor = 1.0 / math.sqrt(data_count * rows * seq_count)
    any_space = pl.BlockSpec(memory_space=pl.ANY)
    vmem = pl.BlockSpec(memory_space=pltpu.VMEM)
    slices = (CHUNKS, CHIPS, SLICE, HD)
    dma = pltpu.SemaphoreType.DMA
    token_grad, proj_grad = pl.pallas_call(
        functools.partial(kernel, scale, factor),
        out_shape=(
            jax.ShapeDtypeStruct((rows, width), BF16),
            jax.ShapeDtypeStruct((4, 3 * INNER), F32),
        ),
        in_specs=[any_space] * 3,
        out_specs=(vmem, vmem),
        scratch_shapes=[
            pltpu.VMEM((ROWS, WIDTH), BF16),
            pltpu.VMEM((ROWS, INNER), BF16),
            pltpu.VMEM((WIDTH, 3 * INNER), BF16),
            pltpu.VMEM((ROWS, 3 * INNER), BF16),
            pltpu.VMEM((WIDTH, ROWS), F32),
            pltpu.VMEM((FLOWS + 1, WIDTH, ROWS), F32),
            pltpu.VMEM((FLOWS, WIDTH, ROWS), F32),
            pltpu.VMEM((WIDTH, 2 * ROWS), BF16),
            pltpu.VMEM((2,) + slices, F32),
            pltpu.VMEM(slices, F32),
            pltpu.VMEM(slices, F32),
            pltpu.VMEM(slices, F32),
            pltpu.VMEM(slices, F32),
            pltpu.VMEM(slices, F32),
            pltpu.VMEM(slices, F32),
            pltpu.VMEM((ROWS, 3 * INNER), F32),
            pltpu.VMEM((2,) + slices, BF16),
            pltpu.VMEM((ROWS, 3 * INNER), BF16),
            pltpu.VMEM((3, HEADS, ROWS, HD), F32),
            pltpu.VMEM((FLOWS, 3, ROWS, HD), F32),
            pltpu.VMEM((FLOWS, GROUPS, 8, HD), F32),
            pltpu.VMEM((FLOWS, GROUPS, 8, HD), F32),
            pltpu.VMEM((FLOWS, 2, 8, HD), F32),
            pltpu.VMEM((FLOWS, 2, 8, HD), F32),
            pltpu.VMEM((FLOWS, OWNERS, 8, HD), F32),
            dma((5,)),
            dma((6,)),
            dma((6,)),
            dma((2 * FLOWS, PIECES)),
            dma((2 * FLOWS, PIECES)),
            dma((CHUNKS, CHIPS - 1)),
            dma((CHUNKS, CHIPS - 1)),
            dma((CHUNKS, CHIPS - 1)),
            dma((CHUNKS, CHIPS - 1)),
            dma((FLOWS, 3)),
            dma((FLOWS, 3)),
            dma((FLOWS, STEPS)),
            dma((FLOWS, STEPS)),
            dma((FLOWS, OWNERS)),
            dma((FLOWS, OWNERS)),
        ],
        compiler_params=pltpu.CompilerParams(
            collective_id=0, has_side_effects=True, vmem_limit_bytes=60 * 1024 * 1024
        ),
    )(tokens.reshape(rows, width), weights, dout.reshape(rows, INNER))
    token_grad, proj_grad = pl.pallas_call(
        settle,
        out_shape=(
            jax.ShapeDtypeStruct((rows, width), BF16),
            jax.ShapeDtypeStruct((4, 3 * INNER), F32),
        ),
        in_specs=[any_space] * 2,
        out_specs=(any_space, any_space),
        scratch_shapes=[
            pltpu.VMEM((rows, width), BF16),
            pltpu.VMEM((4, 3 * INNER), F32),
            dma((2,)),
            dma((2,)),
        ],
    )(token_grad, proj_grad)
    return (token_grad.reshape(1, rows, width), proj_grad)


def solution(mesh):
    in_specs = (P("dp", "seq", None), P(), P("dp", "seq", None))
    out_specs = (P("dp", "seq", None), P(("dp", "seq"), None))
    return jax.shard_map(shards, mesh=mesh, in_specs=in_specs, out_specs=out_specs, check_vma=False)
```

```python
import functools
import math

import jax
import jax.numpy as jnp
from jax import lax
from jax.experimental import pallas as pl
from jax.experimental.pallas import tpu as pltpu
from jax.sharding import PartitionSpec as P

MESH = pl.DeviceIdType.MESH
F32 = jnp.float32
BF16 = jnp.bfloat16

HEADS = 8
HD = 128
ROWS = 128
WIDTH = 1024
INNER = HEADS * HD
NX, NY, NZ = 4, 4, 8
CHIPS = NX * NY
CHUNKS = 2
SLICE = 32
FLOWS = 6
GROUPS = 128
STEPS = 4
OWNERS = 8
PIECES = 4

ORDERS = (
    ("xu", "xv", "yu", "yv", "za", "zb", "zc"),
    ("xv", "xu", "yv", "yu", "za", "zb", "zc"),
    ("yu", "yv", "za", "xu", "xv", "zb", "zc"),
    ("yv", "yu", "zb", "xv", "xu", "za", "zc"),
    ("zb", "za", "xv", "xu", "yv", "yu", "zc"),
    ("za", "zb", "xu", "xv", "yu", "yv", "zc"),
)


def bits_of(x, y, z):
    return {
        "xu": (x % 2 + x // 2) % 2,
        "xv": x // 2,
        "yu": (y % 2 + y // 2) % 2,
        "yv": y // 2,
        "za": (z % 2 + (z // 2) % 2) % 2,
        "zb": (z // 2) % 2,
        "zc": z // 4,
    }


def place_of(flow, bits):
    total = bits[ORDERS[flow][0]]
    for step, name in enumerate(ORDERS[flow][1:]):
        total = total + bits[name] * (GROUPS >> (step + 1))
    return total


SHIFTS = sorted(
    ((dx, dy) for dx in range(NX) for dy in range(NY) if (dx, dy) != (0, 0)),
    key=lambda d: -(min(d[0], NX - d[0]) + min(d[1], NY - d[1])),
)


def dot(a, b, dims):
    return lax.dot_general(a, b, (dims, ((), ())), preferred_element_type=F32)


def kernel(
    scale,
    factor,
    tok_hbm,
    w_hbm,
    g_hbm,
    tg_ref,
    pg_ref,
    tok,
    g,
    w,
    proj,
    tokf,
    tkr,
    tkx,
    tokt,
    loc,
    s1b,
    tb,
    r1,
    eb,
    r2,
    s3b,
    lpart,
    st,
    qg,
    qf,
    qr,
    acc,
    rb,
    fin,
    finp,
    fr,
    load_sem,
    pair_send,
    pair_recv,
    tk_send,
    tk_recv,
    p1_send,
    p1_recv,
    p2_send,
    p2_recv,
    q_send,
    q_recv,
    rs_send,
    rs_recv,
    f_send,
    f_recv,
):
    seq = lax.axis_index("seq")
    z = lax.axis_index("dp")
    core = seq % 2
    chip = seq // 2
    y = chip % NY
    x = chip // NY
    other = 1 - core

    def seq_at(cx, cy):
        return (cx * NY + cy) * 2 + core

    partner = (z, seq + 1 - 2 * core)
    near = {
        "xu": (z, seq_at(x + 1 - 2 * (x % 2), y)),
        "xv": (z, seq_at(3 - x, y)),
        "yu": (z, seq_at(x, y + 1 - 2 * (y % 2))),
        "yv": (z, seq_at(x, 3 - y)),
        "za": (z + 1 - 2 * (z % 2), seq),
        "zb": ((z + 2 * (z % 2) - 1 + NZ) % NZ, seq),
        "zc": ((z + 4) % NZ, seq),
    }
    def crossed(device):
        return (device[0], device[1] + 1 - 2 * core)

    def flipped_place(place, name):
        px, py, pz = place
        if name == "xu":
            return (px + 1 - 2 * (px % 2), py, pz)
        if name == "xv":
            return (3 - px, py, pz)
        if name == "yu":
            return (px, py + 1 - 2 * (py % 2), pz)
        if name == "yv":
            return (px, 3 - py, pz)
        if name == "za":
            return (px, py, pz + 1 - 2 * (pz % 2))
        if name == "zb":
            return (px, py, (pz // 4) * 4 + 3 - pz % 4)
        return (px, py, (pz + 4) % NZ)

    def owners(flow):
        first, left, right = ORDERS[flow][0], ORDERS[flow][5], ORDERS[flow][6]
        found = []
        for mask in range(OWNERS):
            place = (x, y, z)
            for name, on in ((first, mask & 1), (left, mask & 2), (right, mask & 4)):
                if on:
                    place = flipped_place(place, name)
            found.append(place)
        return found

    bits = bits_of(x, y, z)
    targets = []
    for dx, dy in SHIFTS:
        tx, ty = (x + dx) % NX, (y + dy) % NY
        targets.append((tx * NY + ty, (z, seq_at(tx, ty))))

    def remote(src, dst, send, recv, device):
        return pltpu.make_async_remote_copy(
            src_ref=src,
            dst_ref=dst,
            send_sem=send,
            recv_sem=recv,
            device_id=device,
            device_id_type=MESH,
        )

    load_tok = pltpu.make_async_copy(tok_hbm, tok, load_sem.at[0])
    load_g = pltpu.make_async_copy(g_hbm, g, load_sem.at[1])
    load_tok.start()
    load_w = []
    for part in range(3):
        cols = pl.ds(part * INNER, INNER)
        load_w.append(
            pltpu.make_async_copy(w_hbm.at[:, cols], w.at[:, cols], load_sem.at[2 + part])
        )
        load_w[part].start()
    load_g.start()

    barrier = pltpu.get_barrier_semaphore()
    greeted = [partner, near["za"], near["zb"]] + [t[1] for t in targets]
    greeted += [crossed(near[order[0]]) for order in ORDERS]
    for device in greeted:
        pl.semaphore_signal(barrier, inc=1, device_id=device, device_id_type=MESH)

    load_tok.wait()

    def own_transpose(i, carry):
        rows = pl.ds(pl.multiple_of(i * 128, 128), 128)
        flipped = tok[:, rows].astype(F32).T
        tokf[rows, :] = flipped
        tokt[rows, 0:128] = flipped.astype(BF16)
        return carry

    lax.fori_loop(0, WIDTH // 128, own_transpose, 0)

    for part in range(3):
        load_w[part].wait()

        def project(i, carry, part=part):
            cols = pl.ds(pl.multiple_of(part * INNER + i * 256, 256), 256)
            proj[:, cols] = dot(tok[...], w[:, cols], ((1,), (0,))).astype(BF16)
            return carry

        lax.fori_loop(0, INNER // 256, project, 0, unroll=True)
    load_g.wait()

    def head_cols(part, h):
        return pl.ds(pl.multiple_of(part * INNER + h * HD, HD), HD)

    pl.semaphore_wait(barrier, len(greeted))
    piece = WIDTH // PIECES
    tokens_out = {}
    relays = {}

    def send_tokens(flows, part):
        rows = pl.ds(part * piece, piece)
        for flow in flows:
            copy = remote(
                tokf.at[rows],
                tkr.at[flow, rows],
                tk_send.at[flow, part],
                tk_recv.at[flow, part],
                near[ORDERS[flow][0]],
            )
            copy.start()
            tokens_out[flow, part] = copy

    def relay_tokens(flows, part):
        rows = pl.ds(part * piece, piece)
        for flow in flows:
            tokens_out[flow, part].wait_recv()
            copy = remote(
                tkr.at[flow, rows],
                tkx.at[flow, rows],
                tk_send.at[FLOWS + flow, part],
                tk_recv.at[FLOWS + flow, part],
                partner,
            )
            copy.start()
            relays[flow, part] = copy

    z_flows, xy_flows = (4, 5), (0, 1, 2, 3)
    send_tokens(xy_flows, 0)
    for part in range(PIECES):
        send_tokens(z_flows, part)

    pair_state = []
    for chunk in range(CHUNKS):

        for i in range(HEADS // CHUNKS):
            h = 4 * chunk + i
            q = proj[:, head_cols(0, h)]
            k = proj[:, head_cols(1, h)]
            v = proj[:, head_cols(2, h)]
            d = g[:, head_cols(0, h)]
            loc[0, chunk, 4 * i : 4 * i + 4] = dot(k, v, ((0,), (0,))).reshape(4, SLICE, HD)
            loc[1, chunk, 4 * i : 4 * i + 4] = (scale * dot(q, d, ((0,), (0,)))).reshape(4, SLICE, HD)

        copy = remote(
            loc.at[core, chunk],
            s1b.at[chunk],
            pair_send.at[chunk],
            pair_recv.at[chunk],
            partner,
        )
        copy.start()
        pair_state.append(copy)

    first = []
    for chunk in range(CHUNKS):
        pair_state[chunk].wait_recv()
        tb[chunk] = loc[other, chunk] + s1b[chunk]
        copies = []
        for i, (target, device) in enumerate(targets):
            copy = remote(
                tb.at[chunk, target],
                r1.at[chunk, chip],
                p1_send.at[chunk, i],
                p1_recv.at[chunk, i],
                device,
            )
            copy.start()
            copies.append(copy)
        first.append(copies)
        r1[chunk, chip] = tb[chunk, chip]
    send_tokens(xy_flows, 1)
    send_tok = remote(tokf, tkr.at[FLOWS], pair_send.at[4], pair_recv.at[4], partner)
    send_tok.start()

    row = lax.broadcasted_iota(jnp.int32, (ROWS, ROWS), 0)
    col = lax.broadcasted_iota(jnp.int32, (ROWS, ROWS), 1)
    causal = row >= col

    def inside(h, carry):
        q = proj[:, head_cols(0, h)]
        k = proj[:, head_cols(1, h)]
        v = proj[:, head_cols(2, h)]
        d = g[:, head_cols(0, h)]
        sa = jnp.where(causal, dot(d, v, ((1,), (1,))), 0.0).astype(BF16)
        sb = jnp.where(causal, dot(q, k, ((1,), (1,))), 0.0).astype(BF16)
        lpart[:, head_cols(0, h)] = dot(sa, k, ((1,), (0,)))
        lpart[:, head_cols(1, h)] = dot(sa, q, ((0,), (0,)))
        lpart[:, head_cols(2, h)] = dot(sb, d, ((0,), (0,)))
        return carry

    lax.fori_loop(0, HEADS, inside, 0)

    second = []
    for chunk in range(CHUNKS):
        for copy in first[chunk]:
            copy.wait_recv()
        running = jnp.zeros((SLICE, HD), F32)
        for i in range(CHIPS):
            place = core * i + other * (CHIPS - 1 - i)
            eb[chunk, place] = running
            if i < CHIPS - 1:
                running = running + r1[chunk, place]
        copies = []
        for i, (target, device) in enumerate(targets):
            copy = remote(
                eb.at[chunk, target],
                r2.at[chunk, chip],
                p2_send.at[chunk, i],
                p2_recv.at[chunk, i],
                device,
            )
            copy.start()
            copies.append(copy)
        second.append(copies)
        r2[chunk, chip] = eb[chunk, chip]

    send_tokens(xy_flows, 2)
    send_tokens(xy_flows, 3)
    relay_tokens(xy_flows, 0)
    for part in range(PIECES):
        relay_tokens(z_flows, part)
    send_tok.wait_recv()
    tokt[:, 128:256] = tkr[FLOWS].astype(BF16)

    pair_scan = []
    for chunk in range(CHUNKS):
        for copy in second[chunk]:
            copy.wait_recv()
        copy = remote(
            r2.at[chunk],
            s3b.at[chunk],
            pair_send.at[2 + chunk],
            pair_recv.at[2 + chunk],
            partner,
        )
        copy.start()
        pair_scan.append(copy)
        st[other, chunk] = (r2[chunk] + s1b[chunk]).astype(BF16)

    def finish(h):
        q_cols, k_cols, v_cols = (head_cols(part, h) for part in range(3))
        k = proj[:, k_cols]
        v = proj[:, v_cols]
        d = g[:, q_cols]
        at = 4 * (h % 4)
        prefix = st[0, h // 4, at : at + 4].reshape(HD, HD)
        suffix = st[1, h // 4, at : at + 4].reshape(HD, HD)
        dq = scale * (lpart[:, q_cols] + dot(d, prefix, ((1,), (1,))))
        dk = scale * lpart[:, k_cols] + dot(v, suffix, ((1,), (1,)))
        dv = scale * lpart[:, v_cols] + dot(k, suffix, ((1,), (0,)))
        out = [t.astype(BF16) for t in (dq, dk, dv)]
        for part, (cols, t) in enumerate(zip((q_cols, k_cols, v_cols), out)):
            qg[:, cols] = t
            qf[part, h] = t.astype(F32)

    first_bit = [bits[ORDERS[flow][0]] for flow in range(FLOWS)]

    def head_of(flow, at_core, bit):
        return 4 * (flow % 2) + 2 * at_core + bit

    gather = [None] * FLOWS
    for pair in range(2):
        pair_scan[pair].wait_recv()
        st[core, pair] = s3b[pair].astype(BF16)
        for h in range(4):
            finish(4 * pair + h)
        for part in (2, 1, 0):
            flow = 2 * part + pair
            bit = first_bit[flow]
            link = ORDERS[flow][0]
            copies = []
            for i, (at_core, at_bit, device) in enumerate(
                (
                    (core, 1 - bit, near[link]),
                    (other, 1 - bit, crossed(near[link])),
                    (other, bit, partner),
                )
            ):
                copy = remote(
                    qf.at[part, head_of(flow, at_core, at_bit)],
                    qr.at[flow, i],
                    q_send.at[flow, i],
                    q_recv.at[flow, i],
                    device,
                )
                copy.start()
                copies.append(copy)
            gather[flow] = copies

    for part in (1, 2, 3):
        relay_tokens(xy_flows, part)

    def chip_part(pair):
        blocks = []
        for part in range(3):
            flow = 2 * part + pair
            gather[flow][2].wait_recv()
            own = qg[:, head_cols(part, head_of(flow, core, first_bit[flow]))]
            blocks.append(jnp.concatenate([own, qr[flow, 2].astype(BF16)], axis=0))
        rhs = jnp.concatenate(blocks, axis=1)

        for i in range(NZ):
            out = dot(tokt[i * 128 : i * 128 + 128, :], rhs, ((1,), (0,)))
            for part in range(3):
                flow = 2 * part + pair
                for cx in range(NX):
                    for cy in range(NY):
                        at = 8 * (cx * NY + cy)
                        block = out[at : at + 8, part * 128 : part * 128 + 128]
                        acc[flow, place_of(flow, bits_of(cx, cy, i))] = block

    def halving(flow, step, base):
        size = GROUPS >> (step + 1)
        name = ORDERS[flow][step + 1]
        return remote(
            acc.at[flow, pl.ds(base + (1 - bits[name]) * size, size)],
            rb.at[flow, pl.ds(size, size)],
            rs_send.at[flow, step],
            rs_recv.at[flow, step],
            near[name],
        )

    base = [0] * FLOWS
    steps = []
    current = [None] * FLOWS
    flow_order = (2, 0, 4, 5, 3, 1)
    for flow in flow_order:
        if flow in (2, 5):
            chip_part(flow % 2)
        for part in range(PIECES):
            relays[flow, part].wait_recv()
        gather[flow][0].wait_recv()
        gather[flow][1].wait_recv()
        rhs = jnp.concatenate([qr[flow, 0].astype(BF16), qr[flow, 1].astype(BF16)], axis=0)

        for i in range(NZ):
            rows = pl.ds(i * 128, 128)
            lhs = jnp.concatenate(
                [tkr[flow, rows, :].astype(BF16), tkx[flow, rows, :].astype(BF16)], axis=1
            )
            out = dot(lhs, rhs, ((1,), (0,)))
            for cx in range(NX):
                for cy in range(NY):
                    at = 8 * (cx * NY + cy)
                    place = place_of(flow, bits_of(cx, cy, i))
                    acc[flow, place] = acc[flow, place] + out[at : at + 8]

        current[flow] = halving(flow, 0, 0)
        current[flow].start()
        steps.append(current[flow])

    def token_rows(i, carry):
        rows = pl.ds(pl.multiple_of(i * 256, 256), 256)
        tg_ref[:, rows] = dot(qg[...], w[rows, :], ((1,), (1,))).astype(BF16)
        return carry

    lax.fori_loop(0, WIDTH // 256, token_rows, 0)

    def hand_out(flow):
        copies = [None]
        for mask, place in enumerate(owners(flow)):
            if mask:
                copy = remote(
                    acc.at[flow, place_of(flow, bits_of(*place))],
                    fr.at[flow, mask],
                    f_send.at[flow, mask],
                    f_recv.at[flow, mask],
                    (place[2], seq_at(place[0], place[1])),
                )
                copy.start()
                copies.append(copy)
        return copies

    handed = [None] * FLOWS
    for step in range(STEPS):
        size = GROUPS >> (step + 1)
        for flow in flow_order if step + 1 < STEPS else range(FLOWS):
            current[flow].wait_recv()
            base[flow] = base[flow] + bits[ORDERS[flow][step + 1]] * size
            kept = pl.ds(base[flow], size)
            acc[flow, kept] = acc[flow, kept] + rb[flow, size : 2 * size]
            if step + 1 < STEPS:
                current[flow] = halving(flow, step + 1, base[flow])
                current[flow].start()
                steps.append(current[flow])
            else:
                handed[flow] = hand_out(flow)

    for flow in flow_order:
        own = acc[flow, place_of(flow, bits)]
        for copy in handed[flow][1:]:
            copy.wait_recv()
        fin[flow, 0] = (own + fr[flow, 2] + (fr[flow, 4] + fr[flow, 6])) * factor
        fin[flow, 1] = ((fr[flow, 1] + fr[flow, 3]) + (fr[flow, 5] + fr[flow, 7])) * factor

    last = remote(fin, finp, pair_send.at[5], pair_recv.at[5], partner)
    last.start()
    low = core == 0

    def put(at_core, source):
        for flow in range(FLOWS):
            for flip in range(2):
                bit = first_bit[flow] + flip * (1 - 2 * first_bit[flow])
                cols = head_cols(flow // 2, head_of(flow, at_core, bit))
                pg_ref[:, cols] = jnp.where(low, source[flow, flip, 0:4], source[flow, flip, 4:8])

    put(core, fin)
    last.wait_recv()
    put(other, finp)

    for copy in [send_tok, last] + pair_state + pair_scan + steps:
        copy.wait_send()
    for copies in [tokens_out.values(), relays.values()] + first + second:
        for copy in copies:
            copy.wait_send()
    for flow in range(FLOWS):
        for copy in gather[flow] + handed[flow][1:]:
            copy.wait_send()


def settle(tg_in, pg_in, tg_out, pg_out, tg, pg, sem_in, sem_out):
    ins = [
        pltpu.make_async_copy(tg_in, tg, sem_in.at[0]),
        pltpu.make_async_copy(pg_in, pg, sem_in.at[1]),
    ]
    outs = [
        pltpu.make_async_copy(tg, tg_out, sem_out.at[0]),
        pltpu.make_async_copy(pg, pg_out, sem_out.at[1]),
    ]
    for copy in ins:
        copy.start()
    for copy, out in zip(ins, outs):
        copy.wait()
        out.start()
    for out in outs:
        out.wait()


def shards(tokens, weights, dout):
    rows = tokens.shape[1]
    width = tokens.shape[2]
    seq_count = lax.axis_size("seq")
    data_count = lax.axis_size("dp")
    scale = 1.0 / math.sqrt(HD * rows * seq_count)
    factor = 1.0 / math.sqrt(data_count * rows * seq_count)
    any_space = pl.BlockSpec(memory_space=pl.ANY)
    vmem = pl.BlockSpec(memory_space=pltpu.VMEM)
    slices = (CHUNKS, CHIPS, SLICE, HD)
    dma = pltpu.SemaphoreType.DMA
    token_grad, proj_grad = pl.pallas_call(
        functools.partial(kernel, scale, factor),
        out_shape=(
            jax.ShapeDtypeStruct((rows, width), BF16),
            jax.ShapeDtypeStruct((4, 3 * INNER), F32),
        ),
        in_specs=[any_space] * 3,
        out_specs=(vmem, vmem),
        scratch_shapes=[
            pltpu.VMEM((ROWS, WIDTH), BF16),
            pltpu.VMEM((ROWS, INNER), BF16),
            pltpu.VMEM((WIDTH, 3 * INNER), BF16),
            pltpu.VMEM((ROWS, 3 * INNER), BF16),
            pltpu.VMEM((WIDTH, ROWS), F32),
            pltpu.VMEM((FLOWS + 1, WIDTH, ROWS), F32),
            pltpu.VMEM((FLOWS, WIDTH, ROWS), F32),
            pltpu.VMEM((WIDTH, 2 * ROWS), BF16),
            pltpu.VMEM((2,) + slices, F32),
            pltpu.VMEM(slices, F32),
            pltpu.VMEM(slices, F32),
            pltpu.VMEM(slices, F32),
            pltpu.VMEM(slices, F32),
            pltpu.VMEM(slices, F32),
            pltpu.VMEM(slices, F32),
            pltpu.VMEM((ROWS, 3 * INNER), F32),
            pltpu.VMEM((2,) + slices, BF16),
            pltpu.VMEM((ROWS, 3 * INNER), BF16),
            pltpu.VMEM((3, HEADS, ROWS, HD), F32),
            pltpu.VMEM((FLOWS, 3, ROWS, HD), F32),
            pltpu.VMEM((FLOWS, GROUPS, 8, HD), F32),
            pltpu.VMEM((FLOWS, GROUPS, 8, HD), F32),
            pltpu.VMEM((FLOWS, 2, 8, HD), F32),
            pltpu.VMEM((FLOWS, 2, 8, HD), F32),
            pltpu.VMEM((FLOWS, OWNERS, 8, HD), F32),
            dma((5,)),
            dma((6,)),
            dma((6,)),
            dma((2 * FLOWS, PIECES)),
            dma((2 * FLOWS, PIECES)),
            dma((CHUNKS, CHIPS - 1)),
            dma((CHUNKS, CHIPS - 1)),
            dma((CHUNKS, CHIPS - 1)),
            dma((CHUNKS, CHIPS - 1)),
            dma((FLOWS, 3)),
            dma((FLOWS, 3)),
            dma((FLOWS, STEPS)),
            dma((FLOWS, STEPS)),
            dma((FLOWS, OWNERS)),
            dma((FLOWS, OWNERS)),
        ],
        compiler_params=pltpu.CompilerParams(
            collective_id=0, has_side_effects=True, vmem_limit_bytes=60 * 1024 * 1024
        ),
    )(tokens.reshape(rows, width), weights, dout.reshape(rows, INNER))
    token_grad, proj_grad = pl.pallas_call(
        settle,
        out_shape=(
            jax.ShapeDtypeStruct((rows, width), BF16),
            jax.ShapeDtypeStruct((4, 3 * INNER), F32),
        ),
        in_specs=[any_space] * 2,
        out_specs=(any_space, any_space),
        scratch_shapes=[
            pltpu.VMEM((rows, width), BF16),
            pltpu.VMEM((4, 3 * INNER), F32),
            dma((2,)),
            dma((2,)),
        ],
    )(token_grad, proj_grad)
    return (token_grad.reshape(1, rows, width), proj_grad)


def solution(mesh):
    in_specs = (P("dp", "seq", None), P(), P("dp", "seq", None))
    out_specs = (P("dp", "seq", None), P(("dp", "seq"), None))
    return jax.shard_map(shards, mesh=mesh, in_specs=in_specs, out_specs=out_specs, check_vma=False)
```

```python
import functools
import math

import jax
import jax.numpy as jnp
from jax import lax
from jax.experimental import pallas as pl
from jax.experimental.pallas import tpu as pltpu
from jax.sharding import PartitionSpec as P

MESH = pl.DeviceIdType.MESH
F32 = jnp.float32
BF16 = jnp.bfloat16

HEADS = 8
HD = 128
ROWS = 128
WIDTH = 1024
INNER = HEADS * HD
NX, NY, NZ = 4, 4, 8
CHIPS = NX * NY
CHUNKS = 2
SLICE = 32
FLOWS = 6
GROUPS = 128
STEPS = 4
OWNERS = 8
PIECES = 4

ORDERS = (
    ("xu", "xv", "yu", "yv", "za", "zb", "zc"),
    ("xv", "xu", "yv", "yu", "za", "zb", "zc"),
    ("yu", "yv", "za", "xu", "xv", "zb", "zc"),
    ("yv", "yu", "zb", "xv", "xu", "za", "zc"),
    ("zb", "za", "xv", "xu", "yv", "yu", "zc"),
    ("za", "zb", "xu", "xv", "yu", "yv", "zc"),
)


def bits_of(x, y, z):
    return {
        "xu": (x % 2 + x // 2) % 2,
        "xv": x // 2,
        "yu": (y % 2 + y // 2) % 2,
        "yv": y // 2,
        "za": (z % 2 + (z // 2) % 2) % 2,
        "zb": (z // 2) % 2,
        "zc": z // 4,
    }


def place_of(flow, bits):
    total = bits[ORDERS[flow][0]]
    for step, name in enumerate(ORDERS[flow][1:]):
        total = total + bits[name] * (GROUPS >> (step + 1))
    return total


SHIFTS = sorted(
    ((dx, dy) for dx in range(NX) for dy in range(NY) if (dx, dy) != (0, 0)),
    key=lambda d: -(min(d[0], NX - d[0]) + min(d[1], NY - d[1])),
)


def dot(a, b, dims):
    return lax.dot_general(a, b, (dims, ((), ())), preferred_element_type=F32)


def kernel(
    scale,
    factor,
    tok_hbm,
    w_hbm,
    g_hbm,
    tg_ref,
    pg_ref,
    tok,
    g,
    w,
    proj,
    tokf,
    tkr,
    tkx,
    tokt,
    loc,
    s1b,
    tb,
    r1,
    eb,
    r2,
    s3b,
    lpart,
    st,
    qg,
    qf,
    qr,
    acc,
    rb,
    fin,
    finp,
    fr,
    load_sem,
    pair_send,
    pair_recv,
    tk_send,
    tk_recv,
    p1_send,
    p1_recv,
    p2_send,
    p2_recv,
    q_send,
    q_recv,
    rs_send,
    rs_recv,
    f_send,
    f_recv,
):
    seq = lax.axis_index("seq")
    z = lax.axis_index("dp")
    core = seq % 2
    chip = seq // 2
    y = chip % NY
    x = chip // NY
    other = 1 - core

    def seq_at(cx, cy):
        return (cx * NY + cy) * 2 + core

    partner = (z, seq + 1 - 2 * core)
    near = {
        "xu": (z, seq_at(x + 1 - 2 * (x % 2), y)),
        "xv": (z, seq_at(3 - x, y)),
        "yu": (z, seq_at(x, y + 1 - 2 * (y % 2))),
        "yv": (z, seq_at(x, 3 - y)),
        "za": (z + 1 - 2 * (z % 2), seq),
        "zb": ((z + 2 * (z % 2) - 1 + NZ) % NZ, seq),
        "zc": ((z + 4) % NZ, seq),
    }
    def crossed(device):
        return (device[0], device[1] + 1 - 2 * core)

    def flipped_place(place, name):
        px, py, pz = place
        if name == "xu":
            return (px + 1 - 2 * (px % 2), py, pz)
        if name == "xv":
            return (3 - px, py, pz)
        if name == "yu":
            return (px, py + 1 - 2 * (py % 2), pz)
        if name == "yv":
            return (px, 3 - py, pz)
        if name == "za":
            return (px, py, pz + 1 - 2 * (pz % 2))
        if name == "zb":
            return (px, py, (pz // 4) * 4 + 3 - pz % 4)
        return (px, py, (pz + 4) % NZ)

    def owners(flow):
        first, left, right = ORDERS[flow][0], ORDERS[flow][5], ORDERS[flow][6]
        found = []
        for mask in range(OWNERS):
            place = (x, y, z)
            for name, on in ((first, mask & 1), (left, mask & 2), (right, mask & 4)):
                if on:
                    place = flipped_place(place, name)
            found.append(place)
        return found

    bits = bits_of(x, y, z)
    targets = []
    for dx, dy in SHIFTS:
        tx, ty = (x + dx) % NX, (y + dy) % NY
        targets.append((tx * NY + ty, (z, seq_at(tx, ty))))

    def remote(src, dst, send, recv, device):
        return pltpu.make_async_remote_copy(
            src_ref=src,
            dst_ref=dst,
            send_sem=send,
            recv_sem=recv,
            device_id=device,
            device_id_type=MESH,
        )

    load_tok = pltpu.make_async_copy(tok_hbm, tok, load_sem.at[0])
    load_g = pltpu.make_async_copy(g_hbm, g, load_sem.at[1])
    load_tok.start()
    load_w = []
    for part in range(3):
        cols = pl.ds(part * INNER, INNER)
        load_w.append(
            pltpu.make_async_copy(w_hbm.at[:, cols], w.at[:, cols], load_sem.at[2 + part])
        )
        load_w[part].start()
    load_g.start()

    barrier = pltpu.get_barrier_semaphore()
    greeted = [partner, near["za"], near["zb"]] + [t[1] for t in targets]
    greeted += [crossed(near[order[0]]) for order in ORDERS]
    for device in greeted:
        pl.semaphore_signal(barrier, inc=1, device_id=device, device_id_type=MESH)

    load_tok.wait()

    def own_transpose(i, carry):
        rows = pl.ds(pl.multiple_of(i * 128, 128), 128)
        flipped = tok[:, rows].astype(F32).T
        tokf[rows, :] = flipped
        tokt[rows, 0:128] = flipped.astype(BF16)
        return carry

    lax.fori_loop(0, WIDTH // 128, own_transpose, 0)

    for part in range(3):
        load_w[part].wait()

        def project(i, carry, part=part):
            cols = pl.ds(pl.multiple_of(part * INNER + i * 256, 256), 256)
            proj[:, cols] = dot(tok[...], w[:, cols], ((1,), (0,))).astype(BF16)
            return carry

        lax.fori_loop(0, INNER // 256, project, 0, unroll=True)
    load_g.wait()

    def head_cols(part, h):
        return pl.ds(pl.multiple_of(part * INNER + h * HD, HD), HD)

    pl.semaphore_wait(barrier, len(greeted))
    piece = WIDTH // PIECES
    tokens_out = {}
    relays = {}

    def send_tokens(flows, part):
        rows = pl.ds(part * piece, piece)
        for flow in flows:
            copy = remote(
                tokf.at[rows],
                tkr.at[flow, rows],
                tk_send.at[flow, part],
                tk_recv.at[flow, part],
                near[ORDERS[flow][0]],
            )
            copy.start()
            tokens_out[flow, part] = copy

    def relay_tokens(flows, part):
        rows = pl.ds(part * piece, piece)
        for flow in flows:
            tokens_out[flow, part].wait_recv()
            copy = remote(
                tkr.at[flow, rows],
                tkx.at[flow, rows],
                tk_send.at[FLOWS + flow, part],
                tk_recv.at[FLOWS + flow, part],
                partner,
            )
            copy.start()
            relays[flow, part] = copy

    z_flows, xy_flows = (4, 5), (0, 1, 2, 3)
    send_tokens(xy_flows, 0)
    for part in range(PIECES):
        send_tokens(z_flows, part)

    pair_state = []
    for chunk in range(CHUNKS):

        for i in range(HEADS // CHUNKS):
            h = 4 * chunk + i
            q = proj[:, head_cols(0, h)]
            k = proj[:, head_cols(1, h)]
            v = proj[:, head_cols(2, h)]
            d = g[:, head_cols(0, h)]
            loc[0, chunk, 4 * i : 4 * i + 4] = dot(k, v, ((0,), (0,))).reshape(4, SLICE, HD)
            loc[1, chunk, 4 * i : 4 * i + 4] = (scale * dot(q, d, ((0,), (0,)))).reshape(4, SLICE, HD)

        copy = remote(
            loc.at[core, chunk],
            s1b.at[chunk],
            pair_send.at[chunk],
            pair_recv.at[chunk],
            partner,
        )
        copy.start()
        pair_state.append(copy)

    first = []
    for chunk in range(CHUNKS):
        pair_state[chunk].wait_recv()
        tb[chunk] = loc[other, chunk] + s1b[chunk]
        copies = []
        for i, (target, device) in enumerate(targets):
            copy = remote(
                tb.at[chunk, target],
                r1.at[chunk, chip],
                p1_send.at[chunk, i],
                p1_recv.at[chunk, i],
                device,
            )
            copy.start()
            copies.append(copy)
        first.append(copies)
        r1[chunk, chip] = tb[chunk, chip]
    send_tokens(xy_flows, 1)
    send_tok = remote(tokf, tkr.at[FLOWS], pair_send.at[4], pair_recv.at[4], partner)
    send_tok.start()

    row = lax.broadcasted_iota(jnp.int32, (ROWS, ROWS), 0)
    col = lax.broadcasted_iota(jnp.int32, (ROWS, ROWS), 1)
    causal = row >= col

    def inside(h, carry):
        q = proj[:, head_cols(0, h)]
        k = proj[:, head_cols(1, h)]
        v = proj[:, head_cols(2, h)]
        d = g[:, head_cols(0, h)]
        sa = jnp.where(causal, dot(d, v, ((1,), (1,))), 0.0).astype(BF16)
        sb = jnp.where(causal, dot(q, k, ((1,), (1,))), 0.0).astype(BF16)
        lpart[:, head_cols(0, h)] = dot(sa, k, ((1,), (0,)))
        lpart[:, head_cols(1, h)] = dot(sa, q, ((0,), (0,)))
        lpart[:, head_cols(2, h)] = dot(sb, d, ((0,), (0,)))
        return carry

    lax.fori_loop(0, HEADS, inside, 0)

    second = []
    for chunk in range(CHUNKS):
        for copy in first[chunk]:
            copy.wait_recv()
        running = jnp.zeros((SLICE, HD), F32)
        for i in range(CHIPS):
            place = core * i + other * (CHIPS - 1 - i)
            eb[chunk, place] = running
            if i < CHIPS - 1:
                running = running + r1[chunk, place]
        copies = []
        for i, (target, device) in enumerate(targets):
            copy = remote(
                eb.at[chunk, target],
                r2.at[chunk, chip],
                p2_send.at[chunk, i],
                p2_recv.at[chunk, i],
                device,
            )
            copy.start()
            copies.append(copy)
        second.append(copies)
        r2[chunk, chip] = eb[chunk, chip]

    send_tokens(xy_flows, 2)
    send_tokens(xy_flows, 3)
    relay_tokens(xy_flows, 0)
    for part in range(PIECES):
        relay_tokens(z_flows, part)
    send_tok.wait_recv()
    tokt[:, 128:256] = tkr[FLOWS].astype(BF16)

    pair_scan = []
    for chunk in range(CHUNKS):
        for copy in second[chunk]:
            copy.wait_recv()
        copy = remote(
            r2.at[chunk],
            s3b.at[chunk],
            pair_send.at[2 + chunk],
            pair_recv.at[2 + chunk],
            partner,
        )
        copy.start()
        pair_scan.append(copy)
        st[other, chunk] = (r2[chunk] + s1b[chunk]).astype(BF16)

    def finish(h):
        q_cols, k_cols, v_cols = (head_cols(part, h) for part in range(3))
        k = proj[:, k_cols]
        v = proj[:, v_cols]
        d = g[:, q_cols]
        at = 4 * (h % 4)
        prefix = st[0, h // 4, at : at + 4].reshape(HD, HD)
        suffix = st[1, h // 4, at : at + 4].reshape(HD, HD)
        dq = scale * (lpart[:, q_cols] + dot(d, prefix, ((1,), (1,))))
        dk = scale * lpart[:, k_cols] + dot(v, suffix, ((1,), (1,)))
        dv = scale * lpart[:, v_cols] + dot(k, suffix, ((1,), (0,)))
        out = [t.astype(BF16) for t in (dq, dk, dv)]
        for part, (cols, t) in enumerate(zip((q_cols, k_cols, v_cols), out)):
            qg[:, cols] = t
            qf[part, h] = t.astype(F32)

    first_bit = [bits[ORDERS[flow][0]] for flow in range(FLOWS)]

    def head_of(flow, at_core, bit):
        return 4 * (flow % 2) + 2 * at_core + bit

    gather = [None] * FLOWS
    for pair in range(2):
        pair_scan[pair].wait_recv()
        st[core, pair] = s3b[pair].astype(BF16)
        for h in range(4):
            finish(4 * pair + h)
        for part in (2, 1, 0):
            flow = 2 * part + pair
            bit = first_bit[flow]
            link = ORDERS[flow][0]
            copies = []
            for i, (at_core, at_bit, device) in enumerate(
                (
                    (core, 1 - bit, near[link]),
                    (other, 1 - bit, crossed(near[link])),
                    (other, bit, partner),
                )
            ):
                copy = remote(
                    qf.at[part, head_of(flow, at_core, at_bit)],
                    qr.at[flow, i],
                    q_send.at[flow, i],
                    q_recv.at[flow, i],
                    device,
                )
                copy.start()
                copies.append(copy)
            gather[flow] = copies

    for part in (1, 2, 3):
        relay_tokens(xy_flows, part)

    def chip_part(pair):
        blocks = []
        for part in range(3):
            flow = 2 * part + pair
            gather[flow][2].wait_recv()
            own = qg[:, head_cols(part, head_of(flow, core, first_bit[flow]))]
            blocks.append(jnp.concatenate([own, qr[flow, 2].astype(BF16)], axis=0))
        rhs = jnp.concatenate(blocks, axis=1)

        for i in range(NZ):
            out = dot(tokt[i * 128 : i * 128 + 128, :], rhs, ((1,), (0,)))
            for part in range(3):
                flow = 2 * part + pair
                for cx in range(NX):
                    for cy in range(NY):
                        at = 8 * (cx * NY + cy)
                        block = out[at : at + 8, part * 128 : part * 128 + 128]
                        acc[flow, place_of(flow, bits_of(cx, cy, i))] = block

    def halving(flow, step, base):
        size = GROUPS >> (step + 1)
        name = ORDERS[flow][step + 1]
        return remote(
            acc.at[flow, pl.ds(base + (1 - bits[name]) * size, size)],
            rb.at[flow, pl.ds(size, size)],
            rs_send.at[flow, step],
            rs_recv.at[flow, step],
            near[name],
        )

    base = [0] * FLOWS
    steps = []
    current = [None] * FLOWS
    flow_order = (2, 0, 4, 5, 3, 1)
    for flow in flow_order:
        if flow in (2, 5):
            chip_part(flow % 2)
        for part in range(PIECES):
            relays[flow, part].wait_recv()
        gather[flow][0].wait_recv()
        gather[flow][1].wait_recv()
        rhs = jnp.concatenate([qr[flow, 0].astype(BF16), qr[flow, 1].astype(BF16)], axis=0)

        for i in range(NZ):
            rows = pl.ds(i * 128, 128)
            lhs = jnp.concatenate(
                [tkr[flow, rows, :].astype(BF16), tkx[flow, rows, :].astype(BF16)], axis=1
            )
            out = dot(lhs, rhs, ((1,), (0,)))
            for cx in range(NX):
                for cy in range(NY):
                    at = 8 * (cx * NY + cy)
                    place = place_of(flow, bits_of(cx, cy, i))
                    acc[flow, place] = acc[flow, place] + out[at : at + 8]

        current[flow] = halving(flow, 0, 0)
        current[flow].start()
        steps.append(current[flow])

    def token_rows(i, carry):
        rows = pl.ds(pl.multiple_of(i * 256, 256), 256)
        tg_ref[:, rows] = dot(qg[...], w[rows, :], ((1,), (1,))).astype(BF16)
        return carry


    def hand_out(flow):
        copies = [None]
        places = owners(flow)
        for mask in (7, 5, 6, 4, 3, 2, 1):
            if mask:
                place = places[mask]
                copy = remote(
                    acc.at[flow, place_of(flow, bits_of(*place))],
                    fr.at[flow, mask],
                    f_send.at[flow, mask],
                    f_recv.at[flow, mask],
                    (place[2], seq_at(place[0], place[1])),
                )
                copy.start()
                copies.append(copy)
        return copies

    handed = [None] * FLOWS
    for step in range(STEPS):
        token_rows(step, 0)
        size = GROUPS >> (step + 1)
        for flow in flow_order if step + 1 < STEPS else range(FLOWS):
            current[flow].wait_recv()
            base[flow] = base[flow] + bits[ORDERS[flow][step + 1]] * size
            kept = pl.ds(base[flow], size)
            acc[flow, kept] = acc[flow, kept] + rb[flow, size : 2 * size]
            if step + 1 < STEPS:
                current[flow] = halving(flow, step + 1, base[flow])
                current[flow].start()
                steps.append(current[flow])
            else:
                handed[flow] = hand_out(flow)

    for flow in flow_order:
        own = acc[flow, place_of(flow, bits)]
        for copy in handed[flow][1:]:
            copy.wait_recv()
        fin[flow, 0] = (own + fr[flow, 2] + (fr[flow, 4] + fr[flow, 6])) * factor
        fin[flow, 1] = ((fr[flow, 1] + fr[flow, 3]) + (fr[flow, 5] + fr[flow, 7])) * factor

    last = remote(fin, finp, pair_send.at[5], pair_recv.at[5], partner)
    last.start()
    low = core == 0

    def put(at_core, source):
        for flow in range(FLOWS):
            for flip in range(2):
                bit = first_bit[flow] + flip * (1 - 2 * first_bit[flow])
                cols = head_cols(flow // 2, head_of(flow, at_core, bit))
                pg_ref[:, cols] = jnp.where(low, source[flow, flip, 0:4], source[flow, flip, 4:8])

    put(core, fin)
    last.wait_recv()
    put(other, finp)

    for copy in [send_tok, last] + pair_state + pair_scan + steps:
        copy.wait_send()
    for copies in [tokens_out.values(), relays.values()] + first + second:
        for copy in copies:
            copy.wait_send()
    for flow in range(FLOWS):
        for copy in gather[flow] + handed[flow][1:]:
            copy.wait_send()


def settle(tg_in, pg_in, tg_out, pg_out, tg, pg, sem_in, sem_out):
    ins = [
        pltpu.make_async_copy(tg_in, tg, sem_in.at[0]),
        pltpu.make_async_copy(pg_in, pg, sem_in.at[1]),
    ]
    outs = [
        pltpu.make_async_copy(tg, tg_out, sem_out.at[0]),
        pltpu.make_async_copy(pg, pg_out, sem_out.at[1]),
    ]
    for copy in ins:
        copy.start()
    for copy, out in zip(ins, outs):
        copy.wait()
        out.start()
    for out in outs:
        out.wait()


def shards(tokens, weights, dout):
    rows = tokens.shape[1]
    width = tokens.shape[2]
    seq_count = lax.axis_size("seq")
    data_count = lax.axis_size("dp")
    scale = 1.0 / math.sqrt(HD * rows * seq_count)
    factor = 1.0 / math.sqrt(data_count * rows * seq_count)
    any_space = pl.BlockSpec(memory_space=pl.ANY)
    vmem = pl.BlockSpec(memory_space=pltpu.VMEM)
    slices = (CHUNKS, CHIPS, SLICE, HD)
    dma = pltpu.SemaphoreType.DMA
    token_grad, proj_grad = pl.pallas_call(
        functools.partial(kernel, scale, factor),
        out_shape=(
            jax.ShapeDtypeStruct((rows, width), BF16),
            jax.ShapeDtypeStruct((4, 3 * INNER), F32),
        ),
        in_specs=[any_space] * 3,
        out_specs=(vmem, vmem),
        scratch_shapes=[
            pltpu.VMEM((ROWS, WIDTH), BF16),
            pltpu.VMEM((ROWS, INNER), BF16),
            pltpu.VMEM((WIDTH, 3 * INNER), BF16),
            pltpu.VMEM((ROWS, 3 * INNER), BF16),
            pltpu.VMEM((WIDTH, ROWS), F32),
            pltpu.VMEM((FLOWS + 1, WIDTH, ROWS), F32),
            pltpu.VMEM((FLOWS, WIDTH, ROWS), F32),
            pltpu.VMEM((WIDTH, 2 * ROWS), BF16),
            pltpu.VMEM((2,) + slices, F32),
            pltpu.VMEM(slices, F32),
            pltpu.VMEM(slices, F32),
            pltpu.VMEM(slices, F32),
            pltpu.VMEM(slices, F32),
            pltpu.VMEM(slices, F32),
            pltpu.VMEM(slices, F32),
            pltpu.VMEM((ROWS, 3 * INNER), F32),
            pltpu.VMEM((2,) + slices, BF16),
            pltpu.VMEM((ROWS, 3 * INNER), BF16),
            pltpu.VMEM((3, HEADS, ROWS, HD), F32),
            pltpu.VMEM((FLOWS, 3, ROWS, HD), F32),
            pltpu.VMEM((FLOWS, GROUPS, 8, HD), F32),
            pltpu.VMEM((FLOWS, GROUPS, 8, HD), F32),
            pltpu.VMEM((FLOWS, 2, 8, HD), F32),
            pltpu.VMEM((FLOWS, 2, 8, HD), F32),
            pltpu.VMEM((FLOWS, OWNERS, 8, HD), F32),
            dma((5,)),
            dma((6,)),
            dma((6,)),
            dma((2 * FLOWS, PIECES)),
            dma((2 * FLOWS, PIECES)),
            dma((CHUNKS, CHIPS - 1)),
            dma((CHUNKS, CHIPS - 1)),
            dma((CHUNKS, CHIPS - 1)),
            dma((CHUNKS, CHIPS - 1)),
            dma((FLOWS, 3)),
            dma((FLOWS, 3)),
            dma((FLOWS, STEPS)),
            dma((FLOWS, STEPS)),
            dma((FLOWS, OWNERS)),
            dma((FLOWS, OWNERS)),
        ],
        compiler_params=pltpu.CompilerParams(
            collective_id=0, has_side_effects=True, vmem_limit_bytes=60 * 1024 * 1024
        ),
    )(tokens.reshape(rows, width), weights, dout.reshape(rows, INNER))
    token_grad, proj_grad = pl.pallas_call(
        settle,
        out_shape=(
            jax.ShapeDtypeStruct((rows, width), BF16),
            jax.ShapeDtypeStruct((4, 3 * INNER), F32),
        ),
        in_specs=[any_space] * 2,
        out_specs=(any_space, any_space),
        scratch_shapes=[
            pltpu.VMEM((rows, width), BF16),
            pltpu.VMEM((4, 3 * INNER), F32),
            dma((2,)),
            dma((2,)),
        ],
    )(token_grad, proj_grad)
    return (token_grad.reshape(1, rows, width), proj_grad)


def solution(mesh):
    in_specs = (P("dp", "seq", None), P(), P("dp", "seq", None))
    out_specs = (P("dp", "seq", None), P(("dp", "seq"), None))
    return jax.shard_map(shards, mesh=mesh, in_specs=in_specs, out_specs=out_specs, check_vma=False)
```
